32 devices in a mesh: xb: 4 (over z), yb: 8 (over y, x, core).
Axes of the slice: x: 2, y: 2, z: 4, core: 2. Of those that a mesh axis runs over, the one named last changes fastest.
Arguments:
- tracers: float32 [2, 16, 192, 512], P(None, None, 'yb', 'xb'), may hold values from -6 to 6
- velocities: float32 [2, 16, 192, 512], P(None, None, 'yb', 'xb'), may hold values from -0.24 to 0.24
- level_counts: int32 [192, 512], P('yb', 'xb'), may hold values from 0 to 16, as said below
- lateral_diffusivity: float32 [192, 512], P('yb', 'xb'), may hold values from 0.02 to 0.2
- vertical_diffusivity: float32 [192, 512], P('yb', 'xb'), may hold values from 0.1 to 10
- forcing: float32 [192, 512], P('yb', 'xb'), may hold values from -125 to 125
Outputs:
- tracers_new: bfloat16 [2, 16, 192, 512], P(None, None, 'yb', 'xb')
- surface_height: float32 [192, 512], P('yb', 'xb')
The draws below stay inside these ranges and needn't reach their ends.
Inputs may be any that keep to these rules, and one draw needn't show every extreme that they name: level_counts is 0 exactly on land columns, and land is the union of 8 rectangles, each 64 to 128 columns wide (periodic in x) and 24 to 64 rows high; every other column has 1 or more wet levels.
All inputs are finite; a program needn't handle non-finite values.
Results may differ from the reference program's by a relative error of at most 0.001.
Values sent between devices are 32-bit elements; how exact they have to be, the bound alone decides.
A program may use at most 64 MiB of HBM per device.

```python
import math
import jax
import jax.numpy as jnp
from jax import lax

NZ = 16
ITERS = 3
NX = 512
NY = 192


def draw_level_counts(key, part):
    keys = jax.random.split(jax.random.fold_in(key, 29), 5)
    west_edge = jax.random.randint(keys[0], (8,), 0, NX)
    widths = jax.random.randint(keys[1], (8,), NX // 8, NX // 4 + 1)
    south_edge = jax.random.randint(keys[2], (8,), 0, NY)
    heights = jax.random.randint(keys[3], (8,), NY // 8, NY // 3 + 1)
    cols = jnp.arange(NX, dtype=jnp.int32)
    rows = jnp.arange(NY, dtype=jnp.int32)
    inside_x = jnp.mod(cols[None, :] - west_edge[:, None], NX) < widths[:, None]
    inside_y = (rows[None, :] >= south_edge[:, None]) & (rows[None, :] < south_edge[:, None] + heights[:, None])
    land = jnp.any(inside_y[:, :, None] & inside_x[:, None, :], axis=0)
    depths = jax.random.randint(keys[4], (NY, NX), 1, NZ + 1)
    return jnp.where(land, 0, depths).astype(jnp.int32)


def draw_forcing(key, part):
    keys = jax.random.split(jax.random.fold_in(key, 17), 3)
    rows = jnp.arange(NY, dtype=jnp.float32) / NY
    cols = jnp.arange(NX, dtype=jnp.float32) / NX
    row_scale = jnp.exp(jax.random.uniform(keys[1], (NY,), minval=0.0, maxval=math.log(10.0))) / math.sqrt(10.0)
    col_scale = jnp.exp(jax.random.uniform(keys[2], (NX,), minval=0.0, maxval=math.log(10.0))) / math.sqrt(10.0)
    rise = jnp.power(3.0, rows)[:, None] * jnp.power(3.0, cols)[None, :] / 3.0
    base = jnp.clip(jax.random.normal(keys[0], (NY, NX)), -4.0, 4.0)
    field = base * row_scale[:, None] * col_scale[None, :] * rise
    return field.astype(jnp.float32)


def level_of(own_key, shape, cuts, low, top_value):
    def one(dim, parts):
        steps = jax.random.uniform(jax.random.fold_in(jax.random.fold_in(own_key, 6), dim), (parts,), jnp.float32, low / len(cuts), top_value / len(cuts))
        return jnp.repeat(jnp.exp(steps), shape[dim] // parts).reshape((-1,) + (1,) * (len(shape) - dim - 1))

    factor_of = one(*cuts[0])
    for cut in cuts[1:]:
        factor_of = factor_of * one(*cut)
    return factor_of


def bell_draw(rng, dims, scale, limit, pieces=(), held_as=jnp.bfloat16):
    values = scale * jax.random.normal(rng, dims, jnp.float32)
    if pieces:
        values = values * level_of(rng, dims, pieces, -0.22, 0.18)
    return jnp.clip(values, -limit, limit).astype(held_as)


def setup_inputs(seed: int = 0) -> dict:
    splits = jax.random.split(jax.random.key(seed), 7)
    tracers = bell_draw(splits[0], (2, NZ, NY, NX), 1.0, 6.0, ((2, 8), (3, 4)), jnp.float32)
    velocities = jnp.clip(jax.random.uniform(splits[1], (2, NZ, NY, NX), jnp.float32, -0.24, 0.24) * level_of(splits[1], (2, NZ, NY, NX), ((2, 8), (3, 4)), -0.4, 0.0), -0.24, 0.24)
    level_counts = draw_level_counts(jax.random.fold_in(splits[6], 71), 0)
    lateral_diffusivity = jnp.clip(jnp.exp(math.log(0.2) - 2.3025851 * jax.random.uniform(splits[3], (NY, NX), jnp.float32) ** level_of(splits[3], (NY, NX), ((0, 8), (1, 4)), -0.2, 0.2)), 0.02, 0.2)
    vertical_diffusivity = jnp.clip(jnp.exp(math.log(10.0) - 4.6051702 * jax.random.uniform(splits[4], (NY, NX), jnp.float32) ** level_of(splits[4], (NY, NX), ((0, 8), (1, 4)), -0.2, 0.2)), 0.1, 10.0)
    forcing = draw_forcing(jax.random.fold_in(splits[6], 71), 0)
    return {"tracers": tracers, "velocities": velocities, "level_counts": level_counts, "lateral_diffusivity": lateral_diffusivity, "vertical_diffusivity": vertical_diffusivity, "forcing": forcing}


def advect(conc, flow, wet_cells, north_open):
    east_open = wet_cells[:, :, :-1] * wet_cells[:, :, 1:]
    north_faces = wet_cells[:, :-1, :] * wet_cells[:, 1:, :] * north_open[:-1, None]
    east_speed = flow[0][:, :, :-1]
    north_speed = flow[1][:, :-1, :]
    east_flux = east_open * (jnp.maximum(east_speed, 0.0) * conc[..., :, :-1] + jnp.minimum(east_speed, 0.0) * conc[..., :, 1:])
    north_flux = north_faces * (jnp.maximum(north_speed, 0.0) * conc[..., :-1, :] + jnp.minimum(north_speed, 0.0) * conc[..., 1:, :])
    spread = east_flux[..., 1:-1, 1:] - east_flux[..., 1:-1, :-1] + north_flux[..., 1:, 1:-1] - north_flux[..., :-1, 1:-1]
    return wet_cells[:, 1:-1, 1:-1] * (conc[..., 1:-1, 1:-1] - spread)


def mix(conc, wet_cells, north_open, diffusivity):
    east_open = wet_cells[:, :, :-1] * wet_cells[:, :, 1:]
    north_faces = wet_cells[:, :-1, :] * wet_cells[:, 1:, :] * north_open[:-1, None]
    east_coef = 0.5 * (diffusivity[:, :-1] + diffusivity[:, 1:]) * east_open
    north_coef = 0.5 * (diffusivity[:-1, :] + diffusivity[1:, :]) * north_faces
    east_flux = east_coef * (conc[..., :, 1:] - conc[..., :, :-1])
    north_flux = north_coef * (conc[..., 1:, :] - conc[..., :-1, :])
    return conc[..., 1:-1, 1:-1] + east_flux[..., 1:-1, 1:] - east_flux[..., 1:-1, :-1] + north_flux[..., 1:, 1:-1] - north_flux[..., :-1, 1:-1]


def vertical_pass(layers, counts, coef):
    levels = len(layers)
    zero = jnp.zeros_like(coef)
    links = [jnp.where(level + 1.0 < counts, coef, 0.0) for level in range(levels - 1)] + [zero]
    ratios = []
    values = []
    previous_link = zero
    previous_ratio = zero
    previous_value = 0.0
    for level in range(levels):
        upper = links[level]
        pivot = 1.0 + previous_link + upper - previous_link * previous_ratio
        value = (layers[level] + previous_link * previous_value) / pivot
        ratio = upper / pivot
        ratios.append(ratio)
        values.append(value)
        previous_link = upper
        previous_ratio = ratio
        previous_value = value
    result = values[levels - 1]
    output = [result]
    for level in range(levels - 2, -1, -1):
        result = values[level] + ratios[level] * result
        output.insert(0, result)
    return output


def surface_coefs(depth, north_open):
    east_coef = jnp.minimum(depth[:, :-1], depth[:, 1:])
    north_coef = jnp.minimum(depth[:-1, :], depth[1:, :]) * north_open[:-1, None]
    east = east_coef[1:-1, 1:]
    west = east_coef[1:-1, :-1]
    north = north_coef[1:, 1:-1]
    south = north_coef[:-1, 1:-1]
    centre = 0.1 + east + west + north + south
    return centre, east, west, north, south


def surface_apply(padded, coefs):
    centre, east, west, north, south = coefs
    return (centre * padded[1:-1, 1:-1] - east * padded[1:-1, 2:] - west * padded[1:-1, :-2]
            - north * padded[2:, 1:-1] - south * padded[:-2, 1:-1])


def wrap_pad(array, margin):
    pads = [(0, 0)] * (array.ndim - 2) + [(margin, margin), (margin, margin)]
    return jnp.pad(array, pads, mode="wrap")


def reference(tracers, velocities, level_counts, lateral_diffusivity, vertical_diffusivity, forcing):
    counts = level_counts.astype(jnp.float32)
    counts_wide = wrap_pad(counts, 2)
    lateral_wide = wrap_pad(lateral_diffusivity, 2)
    rows = (jnp.arange(NY + 4, dtype=jnp.int32) - 2) % NY
    north_wide = (rows + 1 < NY).astype(jnp.float32)

    def one_level(level):
        conc = lax.dynamic_slice_in_dim(tracers, level, 1, 1)
        flow = lax.dynamic_slice_in_dim(velocities, level, 1, 1)
        wet_cells = (level.astype(jnp.float32) < counts_wide).astype(jnp.float32)[None]
        advected = advect(wrap_pad(conc, 2), wrap_pad(flow, 2), wet_cells, north_wide)
        mixed = mix(advected, wet_cells[:, 1:-1, 1:-1], north_wide[1:-1], lateral_wide[1:-1, 1:-1])
        return mixed[:, 0]

    mixed_levels = lax.map(one_level, jnp.arange(NZ, dtype=jnp.int32))
    layers = [mixed_levels[level] for level in range(NZ)]
    solved = vertical_pass(layers, counts, vertical_diffusivity)
    tracers_new = jnp.stack(solved, axis=1).astype(jnp.bfloat16)
    column_sum = jnp.zeros_like(forcing)
    for level in range(NZ):
        column_sum = column_sum + (solved[level][1] - solved[level][0])
    barotropic_rhs = forcing + column_sum / NZ
    coefs = surface_coefs(wrap_pad(counts / NZ, 1), north_wide[1:-1])
    surface_height = jnp.zeros_like(forcing)
    residual = barotropic_rhs
    direction = barotropic_rhs
    norm_now = jnp.sum(residual * residual)
    for step in range(ITERS):
        image = surface_apply(jnp.pad(direction, 1, mode="wrap"), coefs)
        alpha = norm_now / jnp.sum(direction * image)
        surface_height = surface_height + alpha * direction
        residual = residual - alpha * image
        norm_next = jnp.sum(residual * residual)
        direction = residual + (norm_next / norm_now) * direction
        norm_now = norm_next
    return tracers_new, surface_height
```

```python
import functools

import jax
import jax.numpy as jnp
from jax import lax
from jax.experimental import pallas as pl
from jax.experimental.pallas import tpu as pltpu
from jax.sharding import PartitionSpec as P

ITERS = 3
MESH = pl.DeviceIdType.MESH
SHIFT = 4.1
SCALE = 4.0
DIRECT = 64
NORTH, SOUTH = 0, 1
LEFT, RIGHT = 0, 1


def add_up(terms):
    while len(terms) > 1:
        terms = [sum(terms[i:i + 2][1:], terms[i]) for i in range(0, len(terms), 2)]
    return terms[0]


def inner(a, b, moments):
    return add_up([x * y * moments[i + j] for i, x in enumerate(a) for j, y in enumerate(b)])


def cg_coefficients(moments):
    one = jnp.ones_like(moments[0])
    zero = jnp.zeros_like(one)
    height = [zero] * ITERS
    residual = [one]
    direction = [one]
    norm = moments[0]
    for step in range(ITERS):
        image = [SHIFT * d for d in direction] + [zero]
        for i, d in enumerate(direction):
            image[i + 1] = image[i + 1] + SCALE * d
        alpha = jnp.clip(norm / inner(direction, image, moments), 0.0, 10.0)
        for i, d in enumerate(direction):
            height[i] = height[i] + alpha * d
        if step + 1 < ITERS:
            padded = residual + [zero]
            residual = [p - alpha * m for p, m in zip(padded, image)]
            new = jnp.maximum(inner(residual, residual, moments), 0.0)
            beta = new / norm
            longer = direction + [zero]
            direction = [p + beta * d for p, d in zip(residual, longer)]
            norm = new
    return height


def kernel(
    nx, ny, levels,
    trac, vel, counts_in, lateral_in, vertical_in, forcing_in,
    rounded, out_height,
    c_ext, f_ext, strip_e, strip_w, counts_i, kv, force,
    y_send, y_recv, x_recv, corner_recv, col_recv,
    rhs, r2_x, r2_corner, r2_y, parts,
    values, ratios, inverses, wide_coefs, flat_coefs,
    load_sem, send1, recv1, send2, recv2, send_r, recv_r, ready,
):
    h, lanes = rhs.shape
    ext = h + 8
    mx, my = lax.axis_index("xb"), lax.axis_index("yb")
    east, west = lax.rem(mx + 1, nx), lax.rem(mx + nx - 1, nx)
    north, south = lax.rem(my + 1, ny), lax.rem(my + ny - 1, ny)

    direct = nx * ny <= DIRECT
    me = my * nx + mx

    barrier = pltpu.get_barrier_semaphore()
    near = [(north, mx), (south, mx)]
    far = [(lax.rem(my + d, ny), mx) for d in range(2, ny - 1)]
    peers = near + [(my, lax.rem(mx + d, nx)) for d in range(1, nx)] + far
    loads = [
        pltpu.make_async_copy(trac, c_ext.at[:, :, pl.ds(0, h), :], load_sem.at[0]),
        pltpu.make_async_copy(vel, f_ext.at[:, :, pl.ds(0, h), :], load_sem.at[1]),
        pltpu.make_async_copy(counts_in, counts_i, load_sem.at[2]),
        pltpu.make_async_copy(lateral_in, strip_e.at[2], load_sem.at[3]),
        pltpu.make_async_copy(lateral_in, strip_w.at[2], load_sem.at[4]),
        pltpu.make_async_copy(vertical_in, kv, load_sem.at[5]),
        pltpu.make_async_copy(forcing_in, force, load_sem.at[6]),
    ]
    for load in loads:
        load.start()
    for y, x in peers:
        pl.semaphore_signal(barrier, inc=1, device_id={"xb": x, "yb": y}, device_id_type=MESH)
    for load in loads:
        load.wait()

    lane = lax.broadcasted_iota(jnp.int32, (h, lanes), 1)
    counts_here = counts_i[...].astype(jnp.float32)
    strip_e[1] = counts_here
    strip_w[1] = counts_here

    for n, ref in enumerate((c_ext, f_ext)):
        for t in range(2):
            rows = pl.ds((2 * n + t) * levels, levels)
            y_send[NORTH, rows] = ref[t, :, 0:2, :]
            y_send[SOUTH, rows] = ref[t, :, h - 2:h, :]

    pack_e = jnp.zeros((h, lanes), jnp.float32)
    pack_w = jnp.zeros((h, lanes), jnp.float32)
    pair = lane // 2
    for p in range(4 * levels):
        ref = c_ext if p < 2 * levels else f_ext
        plane = ref[(p // levels) % 2, p % levels, 0:h, :]
        turned = pltpu.roll(plane, (2 * p + 2) % lanes, 1)
        pack_e = jnp.where(pair == p, turned, pack_e)
        pack_w = jnp.where(pair == (p + 1) % (lanes // 2), turned, pack_w)
    pack_w = pltpu.roll(pack_w, lanes - 2, 1)
    strip_e[0] = pack_e
    strip_w[0] = pack_w

    pl.semaphore_wait(barrier, len(peers))

    def remote(src, dst, send, recv, i, y, x):
        return pltpu.make_async_remote_copy(
            src_ref=src, dst_ref=dst, send_sem=send.at[i], recv_sem=recv.at[i],
            device_id={"xb": x, "yb": y}, device_id_type=MESH,
        )

    low, high = pl.ds(0, 8), pl.ds(h - 8, 8)
    cols = pl.ds(1, 2)
    first = [
        remote(strip_e.at[:, high], corner_recv.at[LEFT, SOUTH], send1, recv1, 0, north, east),
        remote(strip_e.at[:, low], corner_recv.at[LEFT, NORTH], send1, recv1, 1, south, east),
        remote(strip_w.at[:, high], corner_recv.at[RIGHT, SOUTH], send1, recv1, 2, north, west),
        remote(strip_w.at[:, low], corner_recv.at[RIGHT, NORTH], send1, recv1, 3, south, west),
        remote(strip_e, x_recv.at[LEFT], send1, recv1, 4, my, east),
        remote(strip_w, x_recv.at[RIGHT], send1, recv1, 5, my, west),
        remote(strip_e.at[cols, high], col_recv.at[SOUTH], send1, recv1, 6, north, mx),
        remote(strip_e.at[cols, low], col_recv.at[NORTH], send1, recv1, 7, south, mx),
        remote(y_send.at[SOUTH], y_recv.at[SOUTH], send1, recv1, 8, north, mx),
        remote(y_send.at[NORTH], y_recv.at[NORTH], send1, recv1, 9, south, mx),
    ]
    for y, x in near:
        pl.semaphore_signal(ready.at[0], inc=1, device_id={"xb": x, "yb": y}, device_id_type=MESH)
    for copy in first[4:]:
        copy.start()
    if direct:
        for y, x in far:
            pl.semaphore_signal(ready.at[1], inc=1, device_id={"xb": x, "yb": y}, device_id_type=MESH)
    pl.semaphore_wait(ready.at[0], len(near))
    for copy in first[:4]:
        copy.start()
    coef = kv[...]
    zero = jnp.zeros_like(coef)
    previous_link = zero
    previous_ratio = zero
    for k in range(levels):
        link = jnp.where(k + 1.0 < counts_here, coef, 0.0) if k + 1 < levels else zero
        inverse = 1.0 / (1.0 + previous_link + link - previous_link * previous_ratio)
        previous_ratio = link * inverse
        previous_link = link
        inverses[k] = inverse
        ratios[k] = previous_ratio
    for copy in first:
        copy.wait()

    half = lax.broadcasted_iota(jnp.int32, (8, lanes), 0) < 4
    row = lax.broadcasted_iota(jnp.int32, (ext, lanes), 0)
    lane = lax.broadcasted_iota(jnp.int32, (ext, lanes), 1)
    beyond = ((row >= h) & (row < h + 4) & (my == ny - 1)) | ((row >= h + 4) & (my == 0))

    def tall(main, from_north, from_south):
        return jnp.concatenate([main, jnp.where(half, from_north, from_south)], axis=0)

    for n, ref in enumerate((c_ext, f_ext)):
        for t in range(2):
            rows = pl.ds((2 * n + t) * levels, levels)
            ref[t, :, h:h + 2, :] = y_recv[NORTH, rows]
            ref[t, :, h + 2:h + 6, :] = jnp.zeros((levels, 4, lanes), jnp.float32)
            ref[t, :, h + 6:h + 8, :] = y_recv[SOUTH, rows]

    def tall_field(i):
        main = tall(strip_e[i], col_recv[NORTH, i - 1], col_recv[SOUTH, i - 1])
        left = tall(x_recv[LEFT, i], corner_recv[LEFT, NORTH, i], corner_recv[LEFT, SOUTH, i])
        right = tall(x_recv[RIGHT, i], corner_recv[RIGHT, NORTH, i], corner_recv[RIGHT, SOUTH, i])
        return main, left, right

    def up(x):
        return pltpu.roll(x, x.shape[0] - 1, 0)

    def down(x):
        return pltpu.roll(x, 1, 0)

    n_main, n_left, n_right = [jnp.where(beyond, 0.0, x) for x in tall_field(1)]
    h_main, h_left, h_right = tall_field(2)

    first_lane = lane == 0
    last_lane = lane == lanes - 1

    def eastward(x, right):
        return jnp.where(last_lane, pltpu.roll(right, lanes - 1, 1), pltpu.roll(x, lanes - 1, 1))

    def westward(x, left):
        return jnp.where(first_lane, pltpu.roll(left, 1, 1), pltpu.roll(x, 1, 1))

    odd = lane % 2 == 1
    blank = jnp.zeros((8, lanes), jnp.float32)
    own_e = jnp.concatenate([strip_e[0], blank], axis=0)
    own_w = jnp.concatenate([strip_w[0], blank], axis=0)
    left = tall(x_recv[LEFT, 0], corner_recv[LEFT, NORTH, 0], corner_recv[LEFT, SOUTH, 0])
    right = tall(x_recv[RIGHT, 0], corner_recv[RIGHT, NORTH, 0], corner_recv[RIGHT, SOUTH, 0])

    def lroll(x, shift):
        return pltpu.roll(x, shift % lanes, 1)

    s_c = jnp.where(odd, left, right)
    s_w = jnp.where(odd, lroll(left, 1), lroll(own_e, -1))
    s_e = jnp.where(odd, lroll(own_w, 1), lroll(right, -1))
    lower = lane < 2 * levels

    def spread(x, n):
        start = 2 * levels * (2 + n)
        return jnp.where(lower, lroll(x, -start), lroll(x, 2 * levels - start))

    s_ue, s_uw, s_v = spread(s_c, 0), spread(s_w, 0), spread(s_c, 1)
    n_c = jnp.where(odd, n_left[:, lanes - 1:], n_right[:, :1])
    n_w = jnp.where(odd, n_left[:, lanes - 2:lanes - 1], n_main[:, lanes - 1:])
    n_e = jnp.where(odd, n_main[:, :1], n_right[:, 1:2])
    rank = ((lane // 2) % levels).astype(jnp.float32)
    s_ue_open = jnp.where(rank < jnp.minimum(n_c, n_e), s_ue, 0.0)
    s_uw_open = jnp.where(rank < jnp.minimum(n_w, n_c), s_uw, 0.0)
    s_v_open = jnp.where(rank < jnp.minimum(n_c, up(n_c)), s_v, 0.0)
    flux_e = jnp.maximum(s_ue_open, 0.0) * s_c + jnp.minimum(s_ue_open, 0.0) * s_e
    flux_w = jnp.maximum(s_uw_open, 0.0) * s_w + jnp.minimum(s_uw_open, 0.0) * s_c
    flux_n = jnp.maximum(s_v_open, 0.0) * s_c + jnp.minimum(s_v_open, 0.0) * up(s_c)
    s_adv = jnp.where(rank < n_c, s_c - (flux_e - flux_w + flux_n - down(flux_n)), 0.0)

    face_e = jnp.minimum(n_main, eastward(n_main, n_right))
    face_w = jnp.minimum(n_main, westward(n_main, n_left))
    face_n = jnp.minimum(n_main, up(n_main))
    face_s = down(face_n)
    mix_e = (0.5 * (h_main + eastward(h_main, h_right)))[:h]
    mix_w = (0.5 * (h_main + westward(h_main, h_left)))[:h]
    mix_n = 0.5 * (h_main + up(h_main))
    mix_s = down(mix_n)[:h]
    mix_n = mix_n[:h]

    def transport(c, edge_c, edge_a, wide, flat):
        stay, ue_neg, uw_pos, vn_neg, vs_pos = wide
        keep, ce, cw, cn, cs = flat
        c_east = jnp.where(last_lane, edge_c, lroll(c, -1))
        c_west = jnp.where(first_lane, edge_c, lroll(c, 1))
        adv = stay * c - ue_neg * c_east + uw_pos * c_west - vn_neg * up(c) + vs_pos * down(c)
        mid = adv[:h]
        a_east = jnp.where(last_lane[:h], edge_a[:h], lroll(mid, -1))
        a_west = jnp.where(first_lane[:h], edge_a[:h], lroll(mid, 1))
        return keep * mid + ce * a_east + cw * a_west + cn * up(adv)[:h] + cs * down(adv)[:h]

    d_c = lroll(s_c, -2 * levels) - s_c
    d_adv = lroll(s_adv, -2 * levels) - s_adv
    previous_link = zero
    previous = zero
    for k in range(levels):
        u = f_ext[0, k]
        v = f_ext[1, k]
        u_west = jnp.where(first_lane, lroll(s_ue, -(2 * k + 1)), lroll(u, 1))
        ue = jnp.where(k < face_e, u, 0.0)
        uw = jnp.where(k < face_w, u_west, 0.0)
        vn = jnp.where(k < face_n, v, 0.0)
        ue_neg = jnp.minimum(ue, 0.0)
        uw_pos = jnp.maximum(uw, 0.0)
        vn_neg = jnp.minimum(vn, 0.0)
        vs = down(vn)
        vs_pos = jnp.maximum(vs, 0.0)
        out = (ue - ue_neg) - (uw - uw_pos) + (vn - vn_neg) - (vs - vs_pos)
        stay = jnp.where(k < n_main, 1.0 - out, 0.0)
        ce = jnp.where(k < face_e[:h], mix_e, 0.0)
        cw = jnp.where(k < face_w[:h], mix_w, 0.0)
        cn = jnp.where(k < face_n[:h], mix_n, 0.0)
        cs = jnp.where(k < face_s[:h], mix_s, 0.0)
        keep = 1.0 - ((ce + cw) + (cn + cs))
        wide = (stay, ue_neg, uw_pos, vn_neg, vs_pos)
        flat = (keep, ce, cw, cn, cs)
        for i in range(5):
            wide_coefs[k, i] = wide[i]
            flat_coefs[k, i] = flat[i]
        c = c_ext[1, k] - c_ext[0, k]
        mixed = transport(c, lroll(d_c, -(2 * k + 1)), lroll(d_adv, -(2 * k + 1)), wide, flat)
        previous = (mixed + previous_link * previous) * inverses[k]
        values[0, k] = previous
        previous_link = jnp.where(k + 1.0 < counts_here, coef, 0.0)

    result = previous
    column_sum = result
    for k in range(levels - 2, -1, -1):
        result = values[0, k] + ratios[k] * result
        column_sum = column_sum + result
    rhs_here = force[...] + column_sum / levels
    rhs[...] = rhs_here

    second = [
        remote(rhs.at[high], r2_corner.at[LEFT, SOUTH], send2, recv2, 0, north, east),
        remote(rhs.at[low], r2_corner.at[LEFT, NORTH], send2, recv2, 1, south, east),
        remote(rhs.at[high], r2_corner.at[RIGHT, SOUTH], send2, recv2, 2, north, west),
        remote(rhs.at[low], r2_corner.at[RIGHT, NORTH], send2, recv2, 3, south, west),
        remote(rhs, r2_x.at[LEFT], send2, recv2, 4, my, east),
        remote(rhs, r2_x.at[RIGHT], send2, recv2, 5, my, west),
        remote(rhs.at[high], r2_y.at[SOUTH], send2, recv2, 6, north, mx),
        remote(rhs.at[low], r2_y.at[NORTH], send2, recv2, 7, south, mx),
    ]
    for copy in second:
        copy.start()

    previous_link = zero
    previous = [zero, zero]
    for k in range(levels):
        wide = [wide_coefs[k, i] for i in range(5)]
        flat = [flat_coefs[k, i] for i in range(5)]
        inverse = inverses[k]
        for t in range(2):
            turn = -(2 * (t * levels + k) + 1)
            mixed = transport(c_ext[t, k], lroll(s_c, turn), lroll(s_adv, turn), wide, flat)
            previous[t] = (mixed + previous_link * previous[t]) * inverse
            values[t, k] = previous[t]
        previous_link = jnp.where(k + 1.0 < counts_here, coef, 0.0)
    for t in range(2):
        result = previous[t]
        rounded[t, levels - 1] = result.astype(jnp.bfloat16)
        for k in range(levels - 2, -1, -1):
            result = values[t, k] + ratios[k] * result
            rounded[t, k] = result.astype(jnp.bfloat16)

    lefty = lane >= lanes // 2

    def side(left_field, right_field):
        return jnp.where(lefty, left_field, right_field)

    def wide_east(x, y):
        a, b = lroll(x, -1), lroll(y, -1)
        return jnp.where(last_lane, b, a), jnp.where(last_lane, a, b)

    def wide_west(x, y):
        a, b = lroll(x, 1), lroll(y, 1)
        return jnp.where(first_lane, b, a), jnp.where(first_lane, a, b)

    scale = 1.0 / (levels * SCALE)
    deep = (n_main * scale, side(n_left, n_right) * scale)
    deep_e = [jnp.minimum(a, b) for a, b in zip(deep, wide_east(*deep))]
    deep_w = wide_west(*deep_e)
    deep_n = [jnp.minimum(a, up(a)) for a in deep]
    deep_s = [down(a) for a in deep_n]
    centre = [
        (0.1 - SHIFT) / SCALE + ((a + b) + (c + d)) for a, b, c, d in zip(deep_e, deep_w, deep_n, deep_s)
    ]

    def apply(field):
        at_e, at_w = wide_east(*field), wide_west(*field)
        return tuple(
            centre[i] * field[i] - deep_e[i] * at_e[i] - deep_w[i] * at_w[i]
            - deep_n[i] * up(field[i]) - deep_s[i] * down(field[i])
            for i in range(2)
        )

    for copy in second:
        copy.wait()
    r_left = tall(r2_x[LEFT], r2_corner[LEFT, NORTH], r2_corner[LEFT, SOUTH])
    r_right = tall(r2_x[RIGHT], r2_corner[RIGHT, NORTH], r2_corner[RIGHT, SOUTH])
    v0 = (tall(rhs_here, r2_y[NORTH], r2_y[SOUTH]), side(r_left, r_right))
    v1 = apply(v0)
    v2 = apply(v1)
    v3 = apply(v2)
    basis = [x[0][:h] for x in (v0, v1, v2, v3)]

    def partial(i, j):
        return jnp.sum(basis[i] * basis[j], axis=0, keepdims=True)

    rows = [partial(m // 2, m - m // 2) for m in range(2 * ITERS)]
    rows.append(jnp.zeros((8 - len(rows), lanes), jnp.float32))
    part = jnp.concatenate(rows, axis=0)
    place = lax.broadcasted_iota(jnp.int32, (8, lanes), 1)
    part = jnp.sum(part, axis=1, keepdims=True)
    part = jnp.where(place == lax.broadcasted_iota(jnp.int32, (8, lanes), 0), part, 0.0)
    part = jnp.sum(part, axis=0, keepdims=True)
    if direct:
        parts[me] = part
        pl.semaphore_wait(ready.at[1], len(far))
        copies = []
        for dy in range(ny):
            for dx in range(nx):
                if dx or dy:
                    y, x = lax.rem(my + dy, ny), lax.rem(mx + dx, nx)
                    copies.append(remote(parts.at[me], parts.at[me], send_r, recv_r, dy * nx + dx, y, x))
        for copy in copies:
            copy.start()
        for copy in copies:
            copy.wait()
        total = add_up([parts[i] for i in range(nx * ny)])
    else:
        parts[mx] = part
        copies = []
        for d in range(1, nx):
            copies.append(remote(parts.at[mx], parts.at[mx], send_r, recv_r, d, my, lax.rem(mx + d, nx)))
        for copy in copies:
            copy.start()
        for copy in copies:
            copy.wait()
        mine = nx + my
        parts[mine] = add_up([parts[i] for i in range(nx)])
        copies = []
        for d in range(1, ny):
            copies.append(remote(parts.at[mine], parts.at[mine], send_r, recv_r, nx + d, lax.rem(my + d, ny), mx))
        for copy in copies:
            copy.start()
        for copy in copies:
            copy.wait()
        total = add_up([parts[nx + i] for i in range(ny)])
    moments = [
        jnp.sum(jnp.where(place[:1] == m, total, 0.0), axis=1, keepdims=True) for m in range(2 * ITERS)
    ]
    weights = cg_coefficients(moments)
    out_height[...] = sum(w * b for w, b in zip(weights, basis))


def write_out(rounded, height, out_tracers, out_height, sem):
    copies = [
        pltpu.make_async_copy(rounded, out_tracers, sem.at[0]),
        pltpu.make_async_copy(height, out_height, sem.at[1]),
    ]
    for copy in copies:
        copy.start()
    for copy in copies:
        copy.wait()


def local(tracers, velocities, level_counts, lateral_diffusivity, vertical_diffusivity, forcing):
    levels = tracers.shape[1]
    h, lanes = forcing.shape
    assert tracers.shape[0] == 2 and 8 * levels == lanes and h % 8 == 0
    nx, ny = lax.axis_size("xb"), lax.axis_size("yb")
    f32 = jnp.float32
    ext = h + 8
    slots = nx * ny if nx * ny <= DIRECT else nx + ny
    dma = pltpu.SemaphoreType.DMA
    vmem = pltpu.VMEM
    held = pl.pallas_call(
        functools.partial(kernel, nx, ny, levels),
        out_shape=(vmem(tracers.shape, jnp.bfloat16), vmem(forcing.shape, f32)),
        in_specs=[pl.BlockSpec(memory_space=pl.ANY)] * 6,
        out_specs=(pl.BlockSpec(memory_space=vmem),) * 2,
        scratch_shapes=[
            vmem((2, levels, ext, lanes), f32),
            vmem((2, levels, ext, lanes), f32),
            vmem((3, h, lanes), f32),
            vmem((3, h, lanes), f32),
            vmem((h, lanes), jnp.int32),
            vmem((h, lanes), f32),
            vmem((h, lanes), f32),
            vmem((2, 4 * levels, 2, lanes), f32),
            vmem((2, 4 * levels, 2, lanes), f32),
            vmem((2, 3, h, lanes), f32),
            vmem((2, 2, 3, 8, lanes), f32),
            vmem((2, 2, 8, lanes), f32),
            vmem((h, lanes), f32),
            vmem((2, h, lanes), f32),
            vmem((2, 2, 8, lanes), f32),
            vmem((2, 8, lanes), f32),
            vmem((slots, 1, lanes), f32),
            vmem((2, levels, h, lanes), f32),
            vmem((levels, h, lanes), f32),
            vmem((levels, h, lanes), f32),
            vmem((levels, 5, ext, lanes), f32),
            vmem((levels, 5, h, lanes), f32),
            dma((7,)),
            dma((10,)), dma((10,)),
            dma((8,)), dma((8,)),
            dma((slots,)), dma((slots,)),
            pltpu.SemaphoreType.REGULAR((2,)),
        ],
        compiler_params=pltpu.CompilerParams(collective_id=0, has_side_effects=True),
        name="ocean_step",
    )(tracers, velocities, level_counts, lateral_diffusivity, vertical_diffusivity, forcing)
    return pl.pallas_call(
        write_out,
        out_shape=(
            jax.ShapeDtypeStruct(tracers.shape, jnp.bfloat16),
            jax.ShapeDtypeStruct(forcing.shape, f32),
        ),
        in_specs=[pl.BlockSpec(memory_space=vmem)] * 2,
        out_specs=(pl.BlockSpec(memory_space=pl.ANY),) * 2,
        scratch_shapes=[dma((2,))],
        name="write_out",
    )(*[pltpu.with_memory_space_constraint(x, vmem) for x in held])


def solution(mesh):
    return jax.shard_map(
        local,
        mesh=mesh,
        in_specs=(
            P(None, None, "yb", "xb"),
            P(None, None, "yb", "xb"),
            P("yb", "xb"),
            P("yb", "xb"),
            P("yb", "xb"),
            P("yb", "xb"),
        ),
        out_specs=(P(None, None, "yb", "xb"), P("yb", "xb")),
        check_vma=False,
    )
```

```python
import functools

import jax
import jax.numpy as jnp
from jax import lax
from jax.experimental import pallas as pl
from jax.experimental.pallas import tpu as pltpu
from jax.sharding import PartitionSpec as P

ITERS = 3
MESH = pl.DeviceIdType.MESH
SHIFT = 4.1
SCALE = 4.0
DIRECT = 64
NORTH, SOUTH = 0, 1
LEFT, RIGHT = 0, 1
TEMP, DIFF, EASTWARD, NORTHWARD = range(4)


def add_up(terms):
    while len(terms) > 1:
        terms = [sum(terms[i:i + 2][1:], terms[i]) for i in range(0, len(terms), 2)]
    return terms[0]


def inner(a, b, moments):
    return add_up([x * y * moments[i + j] for i, x in enumerate(a) for j, y in enumerate(b)])


def cg_coefficients(moments):
    one = jnp.ones_like(moments[0])
    zero = jnp.zeros_like(one)
    height = [zero] * ITERS
    residual = [one]
    direction = [one]
    norm = moments[0]
    for step in range(ITERS):
        image = [SHIFT * d for d in direction] + [zero]
        for i, d in enumerate(direction):
            image[i + 1] = image[i + 1] + SCALE * d
        alpha = jnp.clip(norm / inner(direction, image, moments), 0.0, 10.0)
        for i, d in enumerate(direction):
            height[i] = height[i] + alpha * d
        if step + 1 < ITERS:
            padded = residual + [zero]
            residual = [p - alpha * m for p, m in zip(padded, image)]
            new = jnp.maximum(inner(residual, residual, moments), 0.0)
            beta = new / norm
            longer = direction + [zero]
            direction = [p + beta * d for p, d in zip(residual, longer)]
            norm = new
    return height


def kernel(
    nx, ny, levels,
    trac, vel, counts_in, lateral_in, vertical_in, forcing_in,
    rounded, out_height,
    wide, salt, counts_i, lateral, kv, force,
    strips, corners, y_send, x_recv, corner_recv, y_recv,
    advected, values, ratios, inverses, parts,
    load_sem, send1, recv1, send_r, recv_r, ready,
):
    h, lanes = force.shape
    ext = h + 8
    slots = lanes // levels
    mx, my = lax.axis_index("xb"), lax.axis_index("yb")
    east, west = lax.rem(mx + 1, nx), lax.rem(mx + nx - 1, nx)
    north, south = lax.rem(my + 1, ny), lax.rem(my + ny - 1, ny)

    direct = nx * ny <= DIRECT
    me = my * nx + mx

    barrier = pltpu.get_barrier_semaphore()
    near = [(north, mx), (south, mx)]
    far = [(lax.rem(my + d, ny), mx) for d in range(2, ny - 1)]
    peers = near + [(my, lax.rem(mx + d, nx)) for d in range(1, nx)] + far
    own = pl.ds(0, h)
    loads = [
        pltpu.make_async_copy(trac.at[0], wide.at[TEMP, :, own, :], load_sem.at[0]),
        pltpu.make_async_copy(trac.at[1], salt, load_sem.at[1]),
        pltpu.make_async_copy(vel, wide.at[pl.ds(EASTWARD, 2), :, own, :], load_sem.at[2]),
        pltpu.make_async_copy(counts_in, counts_i, load_sem.at[3]),
        pltpu.make_async_copy(lateral_in, lateral, load_sem.at[4]),
        pltpu.make_async_copy(vertical_in, kv, load_sem.at[5]),
        pltpu.make_async_copy(forcing_in, force, load_sem.at[6]),
    ]
    for load in loads:
        load.start()
    for y, x in peers:
        pl.semaphore_signal(barrier, inc=1, device_id={"xb": x, "yb": y}, device_id_type=MESH)
    for load in loads:
        load.wait()

    def lroll(x, shift):
        return pltpu.roll(x, shift % lanes, 1)

    def up(x):
        return pltpu.roll(x, x.shape[0] - 1, 0)

    def down(x):
        return pltpu.roll(x, 1, 0)

    def turn(x):
        return pltpu.roll(x, 4, 0)

    def spread(x):
        shift = slots
        while shift < lanes:
            x = x + lroll(x, shift)
            shift *= 2
        return x

    half = lax.broadcasted_iota(jnp.int32, (8, lanes), 0) < 4
    fourth = lax.broadcasted_iota(jnp.int32, (8, lanes), 0) == 3
    lane = lax.broadcasted_iota(jnp.int32, (h, lanes), 1)
    slot = lane % slots
    group = lane // slots
    gap = (slot < 2) | (slot >= 6)
    n_own = counts_i[...].astype(jnp.float32)
    h_own = lateral[...]
    f_own = force[...]
    face_e = jnp.minimum(n_own, lroll(n_own, -1))
    face_low = jnp.minimum(n_own[:8], up(n_own[:8]))

    def low_pair(a, b):
        return jnp.where(half, a[:8], turn(b[:8]))

    def high_pair(a, b):
        return jnp.where(half, turn(b[h - 8:]), a[h - 8:])

    pack = [jnp.zeros((h, lanes), jnp.float32)] * 4
    for k in range(levels):
        t = wide[TEMP, k, 0:h, :]
        u = wide[EASTWARD, k, 0:h, :]
        v = wide[NORTHWARD, k, 0:h, :]
        d = salt[k] - t
        wide[DIFF, k, 0:h, :] = d
        flux = jnp.maximum(u, 0.0) * d + jnp.minimum(u, 0.0) * lroll(d, -1)
        u_out = jnp.where(lane == 3, jnp.where(k < face_e, flux, 0.0), u)
        here = group == k
        for i, x in enumerate((t, d, u_out, v)):
            pack[i] = jnp.where(here, lroll(x, slots * k + 4), pack[i])
        flux = jnp.maximum(v[:8], 0.0) * d[:8] + jnp.minimum(v[:8], 0.0) * up(d[:8])
        v_low = jnp.where(fourth, jnp.where(k < face_low, flux, 0.0), v[:8])
        y_send[NORTH, k] = low_pair(d, u)
        y_send[NORTH, levels + k] = low_pair(v_low, t)
        y_send[SOUTH, k] = high_pair(d, u)
        y_send[SOUTH, levels + k] = high_pair(v, t)
    t_own, d_own, u_edge, v_edge = pack
    for i, x in enumerate((n_own, h_own, f_own)):
        a, b = slots * i, slots * (i + 3)
        t_own = jnp.where((group == i) & gap, lroll(x, a + 4), t_own)
        t_own = jnp.where((group == i + 3) & (slot < 2), lroll(x, b + 2), t_own)
        t_own = jnp.where((group == i + 3) & (slot >= 6), lroll(x, b + 6), t_own)
    n_edge = spread(jnp.where(lane < slots, lroll(n_own, 4), 0.0))
    h_edge = spread(jnp.where(lane < slots, lroll(h_own, 4), 0.0))
    western = slot < 4
    sent = [
        [jnp.where(western, d_own, lroll(u_edge, 4)), jnp.where(western, v_edge, lroll(t_own, 4))],
        [jnp.where(western, lroll(u_edge, -4), d_own), jnp.where(western, lroll(t_own, -4), v_edge)],
    ]
    for i, (a, b) in enumerate(sent):
        strips[i, 0] = a
        strips[i, 1] = b
        corners[i, NORTH] = low_pair(a, b)
        corners[i, SOUTH] = high_pair(a, b)
    extra = [(n_own, h_own), (f_own, t_own), (d_own, u_edge), (n_edge, h_edge)]
    for i, (a, b) in enumerate(extra):
        y_send[NORTH, 2 * levels + i] = low_pair(a, b)
        y_send[SOUTH, 2 * levels + i] = high_pair(a, b)

    pl.semaphore_wait(barrier, len(peers))

    def remote(src, dst, send, recv, i, y, x):
        return pltpu.make_async_remote_copy(
            src_ref=src, dst_ref=dst, send_sem=send.at[i], recv_sem=recv.at[i],
            device_id={"xb": x, "yb": y}, device_id_type=MESH,
        )

    for y, x in near:
        pl.semaphore_signal(ready.at[0], inc=1, device_id={"xb": x, "yb": y}, device_id_type=MESH)
    straight = [
        remote(strips.at[0], x_recv.at[LEFT], send1, recv1, 4, my, east),
        remote(strips.at[1], x_recv.at[RIGHT], send1, recv1, 5, my, west),
        remote(y_send.at[SOUTH], y_recv.at[SOUTH], send1, recv1, 6, north, mx),
        remote(y_send.at[NORTH], y_recv.at[NORTH], send1, recv1, 7, south, mx),
    ]
    diagonal = [
        remote(corners.at[0, SOUTH], corner_recv.at[LEFT, SOUTH], send1, recv1, 0, north, east),
        remote(corners.at[0, NORTH], corner_recv.at[LEFT, NORTH], send1, recv1, 1, south, east),
        remote(corners.at[1, SOUTH], corner_recv.at[RIGHT, SOUTH], send1, recv1, 2, north, west),
        remote(corners.at[1, NORTH], corner_recv.at[RIGHT, NORTH], send1, recv1, 3, south, west),
    ]
    for copy in straight:
        copy.start()
    if direct:
        for y, x in far:
            pl.semaphore_signal(ready.at[1], inc=1, device_id={"xb": x, "yb": y}, device_id_type=MESH)
    pl.semaphore_wait(ready.at[0], len(near))
    for copy in diagonal:
        copy.start()

    coef = kv[...]
    zero = jnp.zeros_like(coef)
    previous_link = zero
    previous_ratio = zero
    for k in range(levels):
        link = jnp.where(k + 1.0 < n_own, coef, 0.0) if k + 1 < levels else zero
        inverse = 1.0 / (1.0 + previous_link + link - previous_link * previous_ratio)
        previous_ratio = link * inverse
        previous_link = link
        inverses[k] = inverse
        ratios[k] = previous_ratio

    for copy in straight + diagonal:
        copy.wait()

    row = lax.broadcasted_iota(jnp.int32, (ext, lanes), 0)
    lane = lax.broadcasted_iota(jnp.int32, (ext, lanes), 1)
    slot = lane % slots
    group = lane // slots
    rank = group.astype(jnp.float32)
    western = slot < 4
    first_lane = lane == 0
    last_lane = lane == lanes - 1
    beyond = ((row >= h) & (row < h + 4) & (my == ny - 1)) | ((row >= h + 4) & (my == 0))

    def split(from_north, from_south):
        a = jnp.where(half, from_north, from_south)
        b = turn(jnp.where(half, from_south, from_north))
        return a, b

    def tall(main, halo):
        return jnp.concatenate([main, halo], axis=0)

    for k in range(levels):
        d, u = split(y_recv[NORTH, k], y_recv[SOUTH, k])
        v, t = split(y_recv[NORTH, levels + k], y_recv[SOUTH, levels + k])
        wide[DIFF, k, h:ext, :] = d
        wide[EASTWARD, k, h:ext, :] = u
        wide[NORTHWARD, k, h:ext, :] = v
        wide[TEMP, k, h:ext, :] = t
    halo = [split(y_recv[NORTH, 2 * levels + i], y_recv[SOUTH, 2 * levels + i]) for i in range(len(extra))]
    n_main, h_main = tall(n_own, halo[0][0]), tall(h_own, halo[0][1])
    f_main, t_own = tall(f_own, halo[1][0]), tall(t_own, halo[1][1])
    d_own, u_own = tall(d_own, halo[2][0]), tall(u_edge, halo[2][1])
    n_edge, h_edge = tall(n_edge, halo[3][0]), tall(h_edge, halo[3][1])

    x1, x2 = [], []
    for i in (LEFT, RIGHT):
        a, b = split(corner_recv[i, NORTH], corner_recv[i, SOUTH])
        x1.append(tall(x_recv[i, 0], a))
        x2.append(tall(x_recv[i, 1], b))
    d_side = jnp.where(western, x1[LEFT], x1[RIGHT])
    v_side = jnp.where(western, x2[LEFT], x2[RIGHT])
    u_side = jnp.where(western, lroll(x1[LEFT], -4), lroll(x1[RIGHT], 4))
    t_side = jnp.where(western, lroll(x2[LEFT], -4), lroll(x2[RIGHT], 4))
    fields = jnp.where((slot < 2) | (slot >= 6), t_side, 0.0)
    fields = jnp.where((slot == 2) | (slot == 3), lroll(t_side, 2 - 3 * slots), fields)
    fields = jnp.where((slot == 4) | (slot == 5), lroll(t_side, -2 - 3 * slots), fields)
    n_side = spread(jnp.where((group == 0) & ~beyond, fields, 0.0))
    h_side = spread(jnp.where(group == 1, fields, 0.0))
    f_far = lroll(fields, -2 * slots - 4)
    n_far, h_far = lroll(n_side, -4), lroll(h_side, -4)
    n_main = jnp.where(beyond, 0.0, n_main)
    n_edge = jnp.where(beyond, 0.0, n_edge)

    def to_east(x, y):
        a, b = lroll(x, -1), lroll(y, -1)
        return jnp.where(last_lane, b, a), jnp.where(last_lane, a, b)

    def to_west(x, y):
        a, b = lroll(x, 1), lroll(y, 1)
        return jnp.where(first_lane, b, a), jnp.where(first_lane, a, b)

    n_pair, h_pair = (n_main, n_far), (h_main, h_far)
    face_pair = [jnp.minimum(a, b) for a, b in zip(n_pair, to_east(*n_pair))]
    mix_pair = [0.5 * (a + b) for a, b in zip(h_pair, to_east(*h_pair))]
    face_e, mix_e = face_pair[0], mix_pair[0]
    face_n = jnp.minimum(n_main, up(n_main))
    mix_n = 0.5 * (h_main + up(h_main))

    third, fourth = slot == 3, slot == 4

    def from_east(x, edge):
        return lroll(jnp.where(fourth, edge, x), -1)

    face_side = jnp.minimum(n_side, from_east(n_side, n_edge))
    face_edge = jnp.minimum(n_edge, lroll(n_side, -1))
    face_up = jnp.minimum(n_side, up(n_side))
    open_side = jnp.where(rank < face_side, u_side, 0.0)
    open_edge = jnp.where(rank < face_edge, u_own, 0.0)
    open_up = jnp.where(rank < face_up, v_side, 0.0)

    def upwind(speed, here, there):
        return jnp.maximum(speed, 0.0) * here + jnp.minimum(speed, 0.0) * there

    def advect_side(c, edge):
        flux = upwind(open_side, c, from_east(c, edge))
        flux_edge = upwind(open_edge, edge, lroll(c, -1))
        return flux, flux_edge, upwind(open_up, c, up(c))

    def finish_side(c, flux, flux_edge, flux_n):
        flux_w = lroll(jnp.where(third, flux_edge, flux), 1)
        adv = jnp.where(rank < n_side, c - (flux - flux_w + flux_n - down(flux_n)), 0.0)
        return adv, jnp.where(third, flux_edge, lroll(flux, 1))

    flux, flux_edge, flux_n = advect_side(d_side, d_own)
    flux = jnp.where(slot == slots - 1, u_side, flux)
    adv_side, faces_d = finish_side(d_side, flux, flux_edge, flux_n)

    coef_e = jnp.where(rank < face_side, 0.5 * (h_side + from_east(h_side, h_edge)), 0.0)
    coef_edge = jnp.where(rank < face_edge, 0.5 * (h_edge + lroll(h_side, -1)), 0.0)
    coef_n = jnp.where(rank < face_up, 0.5 * (h_side + up(h_side)), 0.0)
    adv_next = lroll(adv_side, -1)
    flow_e = coef_e * (jnp.where(third, 0.0, adv_next) - adv_side)
    flow_edge = coef_edge * adv_next
    flow_w = lroll(jnp.where(third, flow_edge, flow_e), 1)
    flow_n = coef_n * (up(adv_side) - adv_side)
    mixed = adv_side + (flow_e - flow_w) + (flow_n - down(flow_n))
    mixed = jnp.where(slot == slots - 1, lroll(flow_edge, 4), jnp.where(slot == 0, lroll(flow_e, -3), mixed))
    total = spread(mixed)

    near_face = jnp.where(last_lane, face_pair[1], face_e)
    above = row == h + 3
    column = jnp.zeros((ext, lanes), jnp.float32)
    taken_e, given_e, passed_n = column, column, column
    for k in range(levels):
        d = wide[DIFF, k]
        speed = jnp.where(k < face_e, wide[EASTWARD, k], 0.0)
        edge = lroll(faces_d, -(slots * k + 4))
        flux_e = jnp.where(last_lane, edge, upwind(speed, d, lroll(d, -1)))
        flux_w = jnp.where(first_lane, edge, lroll(flux_e, 1))
        v = wide[NORTHWARD, k]
        flux_n = jnp.where(above, v, upwind(jnp.where(k < face_n, v, 0.0), d, up(d)))
        adv = jnp.where(k < n_main, d - (flux_e - flux_w + flux_n - down(flux_n)), 0.0)
        advected[k] = adv
        column = column + adv
        taken_e = taken_e + jnp.where(k < near_face, lroll(adv, -1), 0.0)
        given_e = given_e + jnp.where(k < face_e, adv, 0.0)
        passed_n = passed_n + jnp.where(k < face_n, up(adv) - adv, 0.0)
    at_edge = mix_pair[1] * taken_e
    given_e = mix_e * given_e
    flow_e = jnp.where(last_lane, total, mix_e * taken_e) - given_e
    flow_w = lroll(jnp.where(last_lane, at_edge, flow_e), 1) + jnp.where(first_lane, total, 0.0)
    flow_n = mix_n * passed_n
    rhs_main = f_main + (column + (flow_e - flow_w) + (flow_n - down(flow_n))) / levels
    rhs_far = lroll(total, -4) + jnp.where(last_lane, at_edge, jnp.where(first_lane, lroll(given_e, 1), 0.0))
    rhs_far = f_far + rhs_far / levels

    scale = 1.0 / (levels * SCALE)
    deep = [scale * x for x in n_pair]
    deep_e = [scale * x for x in face_pair]
    deep_w = to_west(*deep_e)
    deep_n = [jnp.minimum(a, up(a)) for a in deep]
    deep_s = [down(a) for a in deep_n]
    base = (0.1 - SHIFT) / SCALE
    centre = [base + ((a + b) + (c + d)) for a, b, c, d in zip(deep_e, deep_w, deep_n, deep_s)]

    def apply(field):
        at_e, at_w = to_east(*field), to_west(*field)
        return tuple(
            centre[i] * field[i] - deep_e[i] * at_e[i] - deep_w[i] * at_w[i]
            - deep_n[i] * up(field[i]) - deep_s[i] * down(field[i])
            for i in range(2)
        )

    v0 = (rhs_main, rhs_far)
    v1 = apply(v0)
    v2 = apply(v1)
    basis = [x[0][:h] for x in (v0, v1, v2)]
    step_e = v2[0] - to_east(*v2)[0]
    step_n = v2[0] - up(v2[0])
    energy = base * (v2[0] * v2[0]) + deep_e[0] * (step_e * step_e) + deep_n[0] * (step_n * step_n)
    products = [basis[m // 2] * basis[m - m // 2] for m in range(2 * ITERS - 1)] + [energy[:h]]
    rows = [jnp.sum(x, axis=0, keepdims=True) for x in products]
    rows.append(jnp.zeros((8 - len(rows), lanes), jnp.float32))
    part = jnp.concatenate(rows, axis=0)
    place = lax.broadcasted_iota(jnp.int32, (8, lanes), 1)
    part = jnp.sum(part, axis=1, keepdims=True)
    part = jnp.where(place == lax.broadcasted_iota(jnp.int32, (8, lanes), 0), part, 0.0)
    part = jnp.sum(part, axis=0, keepdims=True)

    def tracer_stage():
        flux, flux_edge, flux_n = advect_side(t_side, t_own)
        adv_t, faces_t = finish_side(t_side, flux, flux_edge, flux_n)
        swapped = [jnp.where(third, lroll(x, -1), lroll(x, 1)) for x in (adv_t, adv_side)]
        face_w = to_west(*face_pair)[0][:h]
        mix_w = to_west(*mix_pair)[0][:h]
        mix_s = down(mix_n)[:h]
        face_s = down(face_n)[:h]
        last, first = last_lane[:h], first_lane[:h]
        previous_link = zero
        previous = [zero, zero]
        for k in range(levels):
            t = wide[TEMP, k]
            speed = jnp.where(k < face_e, wide[EASTWARD, k], 0.0)
            edge = lroll(faces_t, -(slots * k + 4))
            flux_e = jnp.where(last_lane, edge, upwind(speed, t, lroll(t, -1)))
            flux_w = jnp.where(first_lane, edge, lroll(flux_e, 1))
            flux_n = upwind(jnp.where(k < face_n, wide[NORTHWARD, k], 0.0), t, up(t))
            adv_main = jnp.where(k < n_main, t - (flux_e - flux_w + flux_n - down(flux_n)), 0.0)
            ce = jnp.where(k < face_e[:h], mix_e[:h], 0.0)
            cw = jnp.where(k < face_w, mix_w, 0.0)
            cn = jnp.where(k < face_n[:h], mix_n[:h], 0.0)
            cs = jnp.where(k < face_s, mix_s, 0.0)
            keep = 1.0 - ((ce + cw) + (cn + cs))
            for i, adv in enumerate((adv_main, advected[k])):
                mid = adv[:h]
                edge = lroll(swapped[i][:h], -(slots * k + 4))
                at_e = jnp.where(last, edge, lroll(mid, -1))
                at_w = jnp.where(first, edge, lroll(mid, 1))
                mixed = keep * mid + ce * at_e + cw * at_w + cn * up(adv)[:h] + cs * down(adv)[:h]
                previous[i] = (mixed + previous_link * previous[i]) * inverses[k]
                values[i, k] = previous[i]
            previous_link = jnp.where(k + 1.0 < n_own, coef, 0.0)
        result = previous
        for k in range(levels - 1, -1, -1):
            if k + 1 < levels:
                result = [values[i, k] + ratios[k] * result[i] for i in range(2)]
            rounded[0, k] = result[0].astype(jnp.bfloat16)
            rounded[1, k] = (result[0] + result[1]).astype(jnp.bfloat16)

    if direct:
        parts[me] = part
        pl.semaphore_wait(ready.at[1], len(far))
        copies = []
        for dy in range(ny):
            for dx in range(nx):
                if dx or dy:
                    y, x = lax.rem(my + dy, ny), lax.rem(mx + dx, nx)
                    copies.append(remote(parts.at[me], parts.at[me], send_r, recv_r, dy * nx + dx, y, x))
        for copy in copies:
            copy.start()
        tracer_stage()
        for copy in copies:
            copy.wait()
        total = add_up([parts[i] for i in range(nx * ny)])
    else:
        parts[mx] = part
        copies = []
        for d in range(1, nx):
            copies.append(remote(parts.at[mx], parts.at[mx], send_r, recv_r, d, my, lax.rem(mx + d, nx)))
        for copy in copies:
            copy.start()
        for copy in copies:
            copy.wait()
        mine = nx + my
        parts[mine] = add_up([parts[i] for i in range(nx)])
        copies = []
        for d in range(1, ny):
            copies.append(remote(parts.at[mine], parts.at[mine], send_r, recv_r, nx + d, lax.rem(my + d, ny), mx))
        for copy in copies:
            copy.start()
        tracer_stage()
        for copy in copies:
            copy.wait()
        total = add_up([parts[nx + i] for i in range(ny)])
    moments = [
        jnp.sum(jnp.where(place[:1] == m, total, 0.0), axis=1, keepdims=True) for m in range(2 * ITERS)
    ]
    weights = cg_coefficients(moments)
    out_height[...] = sum(w * b for w, b in zip(weights, basis))


def write_out(rounded, height, out_tracers, out_height, sem):
    copies = [
        pltpu.make_async_copy(rounded, out_tracers, sem.at[0]),
        pltpu.make_async_copy(height, out_height, sem.at[1]),
    ]
    for copy in copies:
        copy.start()
    for copy in copies:
        copy.wait()


def local(tracers, velocities, level_counts, lateral_diffusivity, vertical_diffusivity, forcing):
    levels = tracers.shape[1]
    h, lanes = forcing.shape
    assert tracers.shape[0] == 2 and 8 * levels == lanes and h % 8 == 0
    nx, ny = lax.axis_size("xb"), lax.axis_size("yb")
    assert nx > 2 and ny > 2
    f32 = jnp.float32
    ext = h + 8
    slots = nx * ny if nx * ny <= DIRECT else nx + ny
    planes = 2 * levels + 4
    dma = pltpu.SemaphoreType.DMA
    vmem = pltpu.VMEM
    held = pl.pallas_call(
        functools.partial(kernel, nx, ny, levels),
        out_shape=(vmem(tracers.shape, jnp.bfloat16), vmem(forcing.shape, f32)),
        in_specs=[pl.BlockSpec(memory_space=pl.ANY)] * 6,
        out_specs=(pl.BlockSpec(memory_space=vmem),) * 2,
        scratch_shapes=[
            vmem((4, levels, ext, lanes), f32),
            vmem((levels, h, lanes), f32),
            vmem((h, lanes), jnp.int32),
            vmem((h, lanes), f32),
            vmem((h, lanes), f32),
            vmem((h, lanes), f32),
            vmem((2, 2, h, lanes), f32),
            vmem((2, 2, 8, lanes), f32),
            vmem((2, planes, 8, lanes), f32),
            vmem((2, 2, h, lanes), f32),
            vmem((2, 2, 8, lanes), f32),
            vmem((2, planes, 8, lanes), f32),
            vmem((levels, ext, lanes), f32),
            vmem((2, levels, h, lanes), f32),
            vmem((levels, h, lanes), f32),
            vmem((levels, h, lanes), f32),
            vmem((slots, 1, lanes), f32),
            dma((7,)),
            dma((8,)), dma((8,)),
            dma((slots,)), dma((slots,)),
            pltpu.SemaphoreType.REGULAR((2,)),
        ],
        compiler_params=pltpu.CompilerParams(collective_id=0, has_side_effects=True),
        name="ocean_step",
    )(tracers, velocities, level_counts, lateral_diffusivity, vertical_diffusivity, forcing)
    return pl.pallas_call(
        write_out,
        out_shape=(
            jax.ShapeDtypeStruct(tracers.shape, jnp.bfloat16),
            jax.ShapeDtypeStruct(forcing.shape, f32),
        ),
        in_specs=[pl.BlockSpec(memory_space=vmem)] * 2,
        out_specs=(pl.BlockSpec(memory_space=pl.ANY),) * 2,
        scratch_shapes=[dma((2,))],
        name="write_out",
    )(*[pltpu.with_memory_space_constraint(x, vmem) for x in held])


def solution(mesh):
    return jax.shard_map(
        local,
        mesh=mesh,
        in_specs=(
            P(None, None, "yb", "xb"),
            P(None, None, "yb", "xb"),
            P("yb", "xb"),
            P("yb", "xb"),
            P("yb", "xb"),
            P("yb", "xb"),
        ),
        out_specs=(P(None, None, "yb", "xb"), P("yb", "xb")),
        check_vma=False,
    )
```

```python
import functools

import jax
import jax.numpy as jnp
from jax import lax
from jax.experimental import pallas as pl
from jax.experimental.pallas import tpu as pltpu
from jax.sharding import PartitionSpec as P

ITERS = 3
MESH = pl.DeviceIdType.MESH
SHIFT = 4.1
SCALE = 4.0
DIRECT = 64
NORTH, SOUTH = 0, 1
LEFT, RIGHT = 0, 1
TEMP, DIFF, EASTWARD, NORTHWARD = range(4)


def add_up(terms):
    while len(terms) > 1:
        terms = [sum(terms[i:i + 2][1:], terms[i]) for i in range(0, len(terms), 2)]
    return terms[0]


def inner(a, b, moments):
    return add_up([x * y * moments[i + j] for i, x in enumerate(a) for j, y in enumerate(b)])


def cg_coefficients(moments):
    one = jnp.ones_like(moments[0])
    zero = jnp.zeros_like(one)
    height = [zero] * ITERS
    residual = [one]
    direction = [one]
    norm = moments[0]
    for step in range(ITERS):
        image = [SHIFT * d for d in direction] + [zero]
        for i, d in enumerate(direction):
            image[i + 1] = image[i + 1] + SCALE * d
        alpha = jnp.clip(norm / inner(direction, image, moments), 0.0, 10.0)
        for i, d in enumerate(direction):
            height[i] = height[i] + alpha * d
        if step + 1 < ITERS:
            padded = residual + [zero]
            residual = [p - alpha * m for p, m in zip(padded, image)]
            new = jnp.maximum(inner(residual, residual, moments), 0.0)
            beta = new / norm
            longer = direction + [zero]
            direction = [p + beta * d for p, d in zip(residual, longer)]
            norm = new
    return height


def kernel(
    nx, ny, levels,
    trac, vel, counts_in, lateral_in, vertical_in, forcing_in,
    rounded, out_height,
    wide, salt, counts_i, lateral, kv, force,
    strips, corners, y_send, late_send, x_recv, corner_recv, y_recv, late_recv,
    advected, values, ratios, inverses, parts,
    load_sem, send1, recv1, send_r, recv_r, ready,
):
    h, lanes = force.shape
    ext = h + 8
    slots = lanes // levels
    mid_level = levels // 2
    mx, my = lax.axis_index("xb"), lax.axis_index("yb")
    east, west = lax.rem(mx + 1, nx), lax.rem(mx + nx - 1, nx)
    north, south = lax.rem(my + 1, ny), lax.rem(my + ny - 1, ny)

    direct = nx * ny <= DIRECT
    me = my * nx + mx

    barrier = pltpu.get_barrier_semaphore()
    near = [(north, mx), (south, mx)]
    far = [(lax.rem(my + d, ny), mx) for d in range(2, ny - 1)]
    peers = near + [(my, lax.rem(mx + d, nx)) for d in range(1, nx)] + far
    own = pl.ds(0, h)
    loads = [
        pltpu.make_async_copy(trac.at[0], wide.at[TEMP, :, own, :], load_sem.at[0]),
        pltpu.make_async_copy(trac.at[1], salt, load_sem.at[1]),
        pltpu.make_async_copy(vel, wide.at[pl.ds(EASTWARD, 2), :, own, :], load_sem.at[2]),
        pltpu.make_async_copy(counts_in, counts_i, load_sem.at[3]),
        pltpu.make_async_copy(lateral_in, lateral, load_sem.at[4]),
        pltpu.make_async_copy(vertical_in, kv, load_sem.at[5]),
        pltpu.make_async_copy(forcing_in, force, load_sem.at[6]),
    ]
    for load in loads:
        load.start()
    for y, x in peers:
        pl.semaphore_signal(barrier, inc=1, device_id={"xb": x, "yb": y}, device_id_type=MESH)

    def clear(side):
        y_recv[side] = jnp.zeros(y_recv.shape[1:], jnp.float32)
        late_recv[side] = jnp.zeros(late_recv.shape[1:], jnp.float32)
        for i in (LEFT, RIGHT):
            corner_recv[i, side] = jnp.zeros(corner_recv.shape[2:], jnp.float32)

    pl.when(my == ny - 1)(lambda: clear(NORTH))
    pl.when(my == 0)(lambda: clear(SOUTH))
    for load in loads:
        load.wait()

    def lroll(x, shift):
        return pltpu.roll(x, shift % lanes, 1)

    def up(x):
        return pltpu.roll(x, x.shape[0] - 1, 0)

    def down(x):
        return pltpu.roll(x, 1, 0)

    def turn(x):
        return pltpu.roll(x, 4, 0)

    def spread(x):
        shift = slots
        while shift < lanes:
            x = x + lroll(x, shift)
            shift *= 2
        return x

    half = lax.broadcasted_iota(jnp.int32, (8, lanes), 0) < 4
    fourth = lax.broadcasted_iota(jnp.int32, (8, lanes), 0) == 3
    lane = lax.broadcasted_iota(jnp.int32, (h, lanes), 1)
    slot = lane % slots
    group = lane // slots
    gap = (slot < 2) | (slot >= 6)
    n_own = counts_i[...].astype(jnp.float32)
    h_own = lateral[...]
    f_own = force[...]
    face_e = jnp.minimum(n_own, lroll(n_own, -1))
    face_low = jnp.minimum(n_own[:8], up(n_own[:8]))

    def low_pair(a, b):
        return jnp.where(half, a[:8], turn(b[:8]))

    def high_pair(a, b):
        return jnp.where(half, turn(b[h - 8:]), a[h - 8:])

    pack = [jnp.zeros((h, lanes), jnp.float32)] * 4
    lows = []
    for k in range(levels):
        t = wide[TEMP, k, 0:h, :]
        u = wide[EASTWARD, k, 0:h, :]
        v = wide[NORTHWARD, k, 0:h, :]
        d = salt[k] - t
        wide[DIFF, k, 0:h, :] = d
        flux = jnp.maximum(u, 0.0) * d + jnp.minimum(u, 0.0) * lroll(d, -1)
        u_out = jnp.where(lane == 3, jnp.where(k < face_e, flux, 0.0), u)
        here = group == k
        for i, x in enumerate((t, d, u_out, v)):
            pack[i] = jnp.where(here, lroll(x, slots * k + 4), pack[i])
        flux = jnp.maximum(v[:8], 0.0) * d[:8] + jnp.minimum(v[:8], 0.0) * up(d[:8])
        v_low = jnp.where(fourth, jnp.where(k < face_low, flux, 0.0), v[:8])
        y_send[NORTH, k] = low_pair(d, u)
        lows.append(v_low)
        y_send[SOUTH, k] = high_pair(d, u)
        if k >= mid_level:
            i = k - mid_level
            y_send[NORTH, levels + i] = low_pair(lows[i], v_low)
            y_send[SOUTH, levels + i] = high_pair(wide[NORTHWARD, i, 0:h, :], v)
            late_send[NORTH, i] = low_pair(wide[TEMP, i, 0:h, :], t)
            late_send[SOUTH, i] = high_pair(wide[TEMP, i, 0:h, :], t)
    t_own, d_own, u_edge, v_edge = pack
    for i, x in enumerate((n_own, h_own, f_own)):
        a, b = slots * i, slots * (i + 3)
        t_own = jnp.where((group == i) & gap, lroll(x, a + 4), t_own)
        t_own = jnp.where((group == i + 3) & (slot < 2), lroll(x, b + 2), t_own)
        t_own = jnp.where((group == i + 3) & (slot >= 6), lroll(x, b + 6), t_own)
    n_edge = spread(jnp.where(lane < slots, lroll(n_own, 4), 0.0))
    h_edge = spread(jnp.where(lane < slots, lroll(h_own, 4), 0.0))
    western = slot < 4
    sent = [
        [jnp.where(western, d_own, lroll(u_edge, 4)), jnp.where(western, v_edge, lroll(t_own, 4))],
        [jnp.where(western, lroll(u_edge, -4), d_own), jnp.where(western, lroll(t_own, -4), v_edge)],
    ]
    for i, (a, b) in enumerate(sent):
        strips[i, 0] = a
        strips[i, 1] = b
        corners[i, NORTH] = low_pair(a, b)
        corners[i, SOUTH] = high_pair(a, b)
    extra = [(n_own, h_own), (f_own, t_own), (d_own, u_edge), (n_edge, h_edge)]
    for i, (a, b) in enumerate(extra):
        y_send[NORTH, levels + mid_level + i] = low_pair(a, b)
        y_send[SOUTH, levels + mid_level + i] = high_pair(a, b)

    pl.semaphore_wait(barrier, len(peers))

    def remote(src, dst, send, recv, i, y, x):
        return pltpu.make_async_remote_copy(
            src_ref=src, dst_ref=dst, send_sem=send.at[i], recv_sem=recv.at[i],
            device_id={"xb": x, "yb": y}, device_id_type=MESH,
        )

    for y, x in near:
        pl.semaphore_signal(ready.at[0], inc=1, device_id={"xb": x, "yb": y}, device_id_type=MESH)
    strip_copies = [
        remote(strips.at[0], x_recv.at[LEFT], send1, recv1, 0, my, east),
        remote(strips.at[1], x_recv.at[RIGHT], send1, recv1, 1, my, west),
    ]
    row_copies = [
        [remote(y_send.at[SOUTH], y_recv.at[SOUTH], send1, recv1, 2, north, mx)],
        [remote(y_send.at[NORTH], y_recv.at[NORTH], send1, recv1, 3, south, mx)],
    ]
    corner_copies = [
        [
            remote(corners.at[0, SOUTH], corner_recv.at[LEFT, SOUTH], send1, recv1, 4, north, east),
            remote(corners.at[1, SOUTH], corner_recv.at[RIGHT, SOUTH], send1, recv1, 5, north, west),
        ],
        [
            remote(corners.at[0, NORTH], corner_recv.at[LEFT, NORTH], send1, recv1, 6, south, east),
            remote(corners.at[1, NORTH], corner_recv.at[RIGHT, NORTH], send1, recv1, 7, south, west),
        ],
    ]
    late_copies = [
        [remote(late_send.at[SOUTH], late_recv.at[SOUTH], send1, recv1, 8, north, mx)],
        [remote(late_send.at[NORTH], late_recv.at[NORTH], send1, recv1, 9, south, mx)],
    ]

    def begin(northward, southward):
        @pl.when(my < ny - 1)
        def _():
            for copy in northward:
                copy.start()

        @pl.when(my > 0)
        def _():
            for copy in southward:
                copy.start()

    def finish(northward, southward):
        @pl.when(my < ny - 1)
        def _():
            for copy in northward:
                copy.wait_send()
            for copy in southward:
                copy.wait_recv()

        @pl.when(my > 0)
        def _():
            for copy in northward:
                copy.wait_recv()
            for copy in southward:
                copy.wait_send()

    begin(*row_copies)
    for copy in strip_copies:
        copy.start()
    if direct:
        for y, x in far:
            pl.semaphore_signal(ready.at[1], inc=1, device_id={"xb": x, "yb": y}, device_id_type=MESH)
    pl.semaphore_wait(ready.at[0], len(near))
    begin(*corner_copies)
    begin(*late_copies)

    coef = kv[...]
    zero = jnp.zeros_like(coef)
    previous_link = zero
    previous_ratio = zero
    for k in range(levels):
        link = jnp.where(k + 1.0 < n_own, coef, 0.0) if k + 1 < levels else zero
        inverse = 1.0 / (1.0 + previous_link + link - previous_link * previous_ratio)
        previous_ratio = link * inverse
        previous_link = link
        inverses[k] = inverse
        ratios[k] = previous_ratio

    finish(*row_copies)

    row = lax.broadcasted_iota(jnp.int32, (ext, lanes), 0)
    lane = lax.broadcasted_iota(jnp.int32, (ext, lanes), 1)
    slot = lane % slots
    group = lane // slots
    rank = group.astype(jnp.float32)
    western = slot < 4
    first_lane = lane == 0
    last_lane = lane == lanes - 1
    beyond = ((row >= h) & (row < h + 4) & (my == ny - 1)) | ((row >= h + 4) & (my == 0))

    def split(from_north, from_south):
        a = jnp.where(half, from_north, from_south)
        b = turn(jnp.where(half, from_south, from_north))
        return a, b

    def tall(main, halo):
        return jnp.concatenate([main, halo], axis=0)

    for k in range(levels):
        d, u = split(y_recv[NORTH, k], y_recv[SOUTH, k])
        wide[DIFF, k, h:ext, :] = d
        wide[EASTWARD, k, h:ext, :] = u
    for k in range(mid_level):
        a, b = split(y_recv[NORTH, levels + k], y_recv[SOUTH, levels + k])
        wide[NORTHWARD, k, h:ext, :] = a
        wide[NORTHWARD, mid_level + k, h:ext, :] = b
    first = levels + mid_level
    halo = [split(y_recv[NORTH, first + i], y_recv[SOUTH, first + i]) for i in range(len(extra))]
    n_main, h_main = tall(n_own, halo[0][0]), tall(h_own, halo[0][1])
    f_main, t_own = tall(f_own, halo[1][0]), tall(t_own, halo[1][1])
    d_own, u_own = tall(d_own, halo[2][0]), tall(u_edge, halo[2][1])
    n_edge, h_edge = tall(n_edge, halo[3][0]), tall(h_edge, halo[3][1])

    n_main = jnp.where(beyond, 0.0, n_main)
    n_edge = jnp.where(beyond, 0.0, n_edge)

    def upwind(speed, here, there):
        return jnp.maximum(speed, 0.0) * here + jnp.minimum(speed, 0.0) * there

    inner_e = jnp.where(last_lane, 0.0, jnp.minimum(n_main, lroll(n_main, -1)))
    inner_mix = 0.5 * (h_main + lroll(h_main, -1))
    face_n = jnp.minimum(n_main, up(n_main))
    mix_n = 0.5 * (h_main + up(h_main))
    above = row == h + 3
    column = jnp.zeros((ext, lanes), jnp.float32)
    passed_e, passed_n, a_own = column, column, column
    for k in range(levels):
        d = wide[DIFF, k]
        flux_e = upwind(jnp.where(k < inner_e, wide[EASTWARD, k], 0.0), d, lroll(d, -1))
        v = wide[NORTHWARD, k]
        flux_n = jnp.where(above, v, upwind(jnp.where(k < face_n, v, 0.0), d, up(d)))
        adv = jnp.where(k < n_main, d - (flux_e - lroll(flux_e, 1) + flux_n - down(flux_n)), 0.0)
        advected[k] = adv
        column = column + adv
        passed_e = passed_e + jnp.where(k < inner_e, lroll(adv, -1) - adv, 0.0)
        passed_n = passed_n + jnp.where(k < face_n, up(adv) - adv, 0.0)
        a_own = jnp.where(group == k, lroll(adv, slots * k + 4), a_own)
    flow_e = inner_mix * passed_e
    flow_n = mix_n * passed_n
    mixed_main = column + (flow_e - lroll(flow_e, 1)) + (flow_n - down(flow_n))

    third, fourth = slot == 3, slot == 4
    coef_own = jnp.where(rank < jnp.minimum(n_edge, lroll(n_edge, -1)), 0.5 * (h_edge + lroll(h_edge, -1)), 0.0)
    coef_own_n = jnp.where(rank < jnp.minimum(n_edge, up(n_edge)), 0.5 * (h_edge + up(h_edge)), 0.0)

    for copy in strip_copies:
        copy.wait()
    finish(*corner_copies)

    x1, x2 = [], []
    for i in (LEFT, RIGHT):
        a, b = split(corner_recv[i, NORTH], corner_recv[i, SOUTH])
        x1.append(tall(x_recv[i, 0], a))
        x2.append(tall(x_recv[i, 1], b))
    d_side = jnp.where(western, x1[LEFT], x1[RIGHT])
    v_side = jnp.where(western, x2[LEFT], x2[RIGHT])
    u_side = jnp.where(western, lroll(x1[LEFT], -4), lroll(x1[RIGHT], 4))
    t_side = jnp.where(western, lroll(x2[LEFT], -4), lroll(x2[RIGHT], 4))
    fields = jnp.where((slot < 2) | (slot >= 6), t_side, 0.0)
    fields = jnp.where((slot == 2) | (slot == 3), lroll(t_side, 2 - 3 * slots), fields)
    fields = jnp.where((slot == 4) | (slot == 5), lroll(t_side, -2 - 3 * slots), fields)
    n_side = spread(jnp.where((group == 0) & ~beyond, fields, 0.0))
    h_side = spread(jnp.where(group == 1, fields, 0.0))
    f_far = lroll(fields, -2 * slots - 4)
    n_far, h_far = lroll(n_side, -4), lroll(h_side, -4)

    def to_east(x, y):
        a, b = lroll(x, -1), lroll(y, -1)
        return jnp.where(last_lane, b, a), jnp.where(last_lane, a, b)

    def to_west(x, y):
        a, b = lroll(x, 1), lroll(y, 1)
        return jnp.where(first_lane, b, a), jnp.where(first_lane, a, b)

    n_pair, h_pair = (n_main, n_far), (h_main, h_far)
    face_pair = [jnp.minimum(a, b) for a, b in zip(n_pair, to_east(*n_pair))]

    def from_east(x, edge):
        return lroll(jnp.where(fourth, edge, x), -1)

    face_side = jnp.minimum(n_side, from_east(n_side, n_edge))
    face_edge = jnp.minimum(n_edge, lroll(n_side, -1))
    face_up = jnp.minimum(n_side, up(n_side))
    open_side = jnp.where(rank < face_side, u_side, 0.0)
    open_edge = jnp.where(rank < face_edge, u_own, 0.0)
    open_up = jnp.where(rank < face_up, v_side, 0.0)

    def advect_side(c, edge):
        flux = upwind(open_side, c, from_east(c, edge))
        flux_edge = upwind(open_edge, edge, lroll(c, -1))
        return flux, flux_edge, upwind(open_up, c, up(c))

    def finish_side(c, flux, flux_edge, flux_n):
        flux_w = lroll(jnp.where(third, flux_edge, flux), 1)
        adv = jnp.where(rank < n_side, c - (flux - flux_w + flux_n - down(flux_n)), 0.0)
        return adv, jnp.where(third, flux_edge, jnp.where(fourth, lroll(flux, 1), 0.0))

    flux, flux_edge, flux_n = advect_side(d_side, d_own)
    flux = jnp.where(slot == slots - 1, u_side, flux)
    adv_side, faces_d = finish_side(d_side, flux, flux_edge, flux_n)

    coef_e = jnp.where(rank < face_side, 0.5 * (h_side + from_east(h_side, h_edge)), 0.0)
    coef_edge = jnp.where(rank < face_edge, 0.5 * (h_edge + lroll(h_side, -1)), 0.0)
    coef_n = jnp.where(rank < face_up, 0.5 * (h_side + up(h_side)), 0.0)
    gained = jnp.where(rank < n_edge, jnp.where(third, -faces_d, faces_d), 0.0)
    a_own = a_own + gained
    flow_e = coef_e * (from_east(adv_side, a_own) - adv_side)
    flow_edge = coef_edge * (lroll(adv_side, -1) - a_own)
    flow_w = lroll(jnp.where(third, flow_edge, flow_e), 1)
    flow_n = coef_n * (up(adv_side) - adv_side)
    mixed = adv_side + (flow_e - flow_w) + (flow_n - down(flow_n))
    inner = coef_own * jnp.where(slot == 2, lroll(gained, -1), jnp.where(fourth, -gained, 0.0))
    flow_w = lroll(jnp.where(third, flow_e, inner), 1)
    flow_n = coef_own_n * (up(gained) - gained)
    mixed_own = gained + (jnp.where(third, flow_edge, inner) - flow_w) + (flow_n - down(flow_n))
    rhs_far = lroll(spread(mixed), -4)
    added = lroll(spread(mixed_own), -4)
    rhs_main = f_main + (mixed_main + jnp.where((lane >= lanes - 2) | (lane < 2), added, 0.0)) / levels
    rhs_far = f_far + rhs_far / levels

    scale = 1.0 / (levels * SCALE)
    deep = [scale * x for x in n_pair]
    deep_e = [scale * x for x in face_pair]
    deep_w = to_west(*deep_e)
    deep_n = [jnp.minimum(a, up(a)) for a in deep]
    deep_s = [down(a) for a in deep_n]
    base = (0.1 - SHIFT) / SCALE
    centre = [base + ((a + b) + (c + d)) for a, b, c, d in zip(deep_e, deep_w, deep_n, deep_s)]

    def apply(field):
        at_e, at_w = to_east(*field), to_west(*field)
        return tuple(
            centre[i] * field[i] - deep_e[i] * at_e[i] - deep_w[i] * at_w[i]
            - deep_n[i] * up(field[i]) - deep_s[i] * down(field[i])
            for i in range(2)
        )

    v0 = (rhs_main, rhs_far)
    v1 = apply(v0)
    v2 = apply(v1)
    basis = [x[0][:h] for x in (v0, v1, v2)]
    step_e = v2[0] - to_east(*v2)[0]
    step_n = v2[0] - up(v2[0])
    energy = base * (v2[0] * v2[0]) + deep_e[0] * (step_e * step_e) + deep_n[0] * (step_n * step_n)
    products = [basis[m // 2] * basis[m - m // 2] for m in range(2 * ITERS - 1)] + [energy[:h]]
    rows = [jnp.sum(x, axis=0, keepdims=True) for x in products]
    rows.append(jnp.zeros((8 - len(rows), lanes), jnp.float32))
    part = jnp.concatenate(rows, axis=0)
    place = lax.broadcasted_iota(jnp.int32, (8, lanes), 1)
    part = jnp.sum(part, axis=1, keepdims=True)
    part = jnp.where(place == lax.broadcasted_iota(jnp.int32, (8, lanes), 0), part, 0.0)
    part = jnp.sum(part, axis=0, keepdims=True)

    def tracer_stage():
        finish(*late_copies)
        for k in range(mid_level):
            a, b = split(late_recv[NORTH, k], late_recv[SOUTH, k])
            wide[TEMP, k, h:ext, :] = a
            wide[TEMP, mid_level + k, h:ext, :] = b
        flux, flux_edge, flux_n = advect_side(t_side, t_own)
        adv_t, faces_t = finish_side(t_side, flux, flux_edge, flux_n)
        mix_pair = [0.5 * (a + b) for a, b in zip(h_pair, to_east(*h_pair))]
        face_e, mix_e = face_pair[0], mix_pair[0]
        rim = first_lane | last_lane
        swapped = [jnp.where(third, lroll(x, -1), lroll(x, 1)) for x in (adv_t, adv_side)]
        face_w = to_west(*face_pair)[0][:h]
        mix_w = to_west(*mix_pair)[0][:h]
        mix_s = down(mix_n)[:h]
        face_s = down(face_n)[:h]
        last, first = last_lane[:h], first_lane[:h]
        previous_link = zero
        previous = [zero, zero]
        for k in range(levels):
            t = wide[TEMP, k]
            speed = jnp.where(k < face_e, wide[EASTWARD, k], 0.0)
            edge = lroll(faces_t, -(slots * k + 4))
            flux_e = jnp.where(last_lane, edge, upwind(speed, t, lroll(t, -1)))
            flux_w = jnp.where(first_lane, edge, lroll(flux_e, 1))
            flux_n = upwind(jnp.where(k < face_n, wide[NORTHWARD, k], 0.0), t, up(t))
            adv_main = jnp.where(k < n_main, t - (flux_e - flux_w + flux_n - down(flux_n)), 0.0)
            ce = jnp.where(k < face_e[:h], mix_e[:h], 0.0)
            cw = jnp.where(k < face_w, mix_w, 0.0)
            cn = jnp.where(k < face_n[:h], mix_n[:h], 0.0)
            cs = jnp.where(k < face_s, mix_s, 0.0)
            keep = 1.0 - ((ce + cw) + (cn + cs))
            adv_d = jnp.where(rim, lroll(a_own, -(slots * k + 4)), advected[k])
            for i, adv in enumerate((adv_main, adv_d)):
                mid = adv[:h]
                edge = lroll(swapped[i][:h], -(slots * k + 4))
                at_e = jnp.where(last, edge, lroll(mid, -1))
                at_w = jnp.where(first, edge, lroll(mid, 1))
                mixed = keep * mid + ce * at_e + cw * at_w + cn * up(adv)[:h] + cs * down(adv)[:h]
                previous[i] = (mixed + previous_link * previous[i]) * inverses[k]
                values[i, k] = previous[i]
            previous_link = jnp.where(k + 1.0 < n_own, coef, 0.0)
        result = previous
        for k in range(levels - 1, -1, -1):
            if k + 1 < levels:
                result = [values[i, k] + ratios[k] * result[i] for i in range(2)]
            rounded[0, k] = result[0].astype(jnp.bfloat16)
            rounded[1, k] = (result[0] + result[1]).astype(jnp.bfloat16)

    if direct:
        parts[me] = part
        pl.semaphore_wait(ready.at[1], len(far))
        copies = []
        for dy in range(ny):
            for dx in range(nx):
                if dx or dy:
                    y, x = lax.rem(my + dy, ny), lax.rem(mx + dx, nx)
                    copies.append(remote(parts.at[me], parts.at[me], send_r, recv_r, dy * nx + dx, y, x))
        for copy in copies:
            copy.start()
        tracer_stage()
        for copy in copies:
            copy.wait()
        total = add_up([parts[i] for i in range(nx * ny)])
    else:
        parts[mx] = part
        copies = []
        for d in range(1, nx):
            copies.append(remote(parts.at[mx], parts.at[mx], send_r, recv_r, d, my, lax.rem(mx + d, nx)))
        for copy in copies:
            copy.start()
        for copy in copies:
            copy.wait()
        mine = nx + my
        parts[mine] = add_up([parts[i] for i in range(nx)])
        copies = []
        for d in range(1, ny):
            copies.append(remote(parts.at[mine], parts.at[mine], send_r, recv_r, nx + d, lax.rem(my + d, ny), mx))
        for copy in copies:
            copy.start()
        tracer_stage()
        for copy in copies:
            copy.wait()
        total = add_up([parts[nx + i] for i in range(ny)])
    moments = [
        jnp.sum(jnp.where(place[:1] == m, total, 0.0), axis=1, keepdims=True) for m in range(2 * ITERS)
    ]
    weights = cg_coefficients(moments)
    out_height[...] = sum(w * b for w, b in zip(weights, basis))


def write_out(rounded, height, out_tracers, out_height, sem):
    copies = [
        pltpu.make_async_copy(rounded, out_tracers, sem.at[0]),
        pltpu.make_async_copy(height, out_height, sem.at[1]),
    ]
    for copy in copies:
        copy.start()
    for copy in copies:
        copy.wait()


def local(tracers, velocities, level_counts, lateral_diffusivity, vertical_diffusivity, forcing):
    levels = tracers.shape[1]
    h, lanes = forcing.shape
    assert tracers.shape[0] == 2 and 8 * levels == lanes and h % 8 == 0
    nx, ny = lax.axis_size("xb"), lax.axis_size("yb")
    assert nx > 2 and ny > 2
    f32 = jnp.float32
    ext = h + 8
    slots = nx * ny if nx * ny <= DIRECT else nx + ny
    planes = levels + levels // 2 + 4
    dma = pltpu.SemaphoreType.DMA
    vmem = pltpu.VMEM
    held = pl.pallas_call(
        functools.partial(kernel, nx, ny, levels),
        out_shape=(vmem(tracers.shape, jnp.bfloat16), vmem(forcing.shape, f32)),
        in_specs=[pl.BlockSpec(memory_space=pl.ANY)] * 6,
        out_specs=(pl.BlockSpec(memory_space=vmem),) * 2,
        scratch_shapes=[
            vmem((4, levels, ext, lanes), f32),
            vmem((levels, h, lanes), f32),
            vmem((h, lanes), jnp.int32),
            vmem((h, lanes), f32),
            vmem((h, lanes), f32),
            vmem((h, lanes), f32),
            vmem((2, 2, h, lanes), f32),
            vmem((2, 2, 8, lanes), f32),
            vmem((2, planes, 8, lanes), f32),
            vmem((2, levels // 2, 8, lanes), f32),
            vmem((2, 2, h, lanes), f32),
            vmem((2, 2, 8, lanes), f32),
            vmem((2, planes, 8, lanes), f32),
            vmem((2, levels // 2, 8, lanes), f32),
            vmem((levels, ext, lanes), f32),
            vmem((2, levels, h, lanes), f32),
            vmem((levels, h, lanes), f32),
            vmem((levels, h, lanes), f32),
            vmem((slots, 1, lanes), f32),
            dma((7,)),
            dma((10,)), dma((10,)),
            dma((slots,)), dma((slots,)),
            pltpu.SemaphoreType.REGULAR((2,)),
        ],
        compiler_params=pltpu.CompilerParams(collective_id=0, has_side_effects=True),
        name="ocean_step",
    )(tracers, velocities, level_counts, lateral_diffusivity, vertical_diffusivity, forcing)
    return pl.pallas_call(
        write_out,
        out_shape=(
            jax.ShapeDtypeStruct(tracers.shape, jnp.bfloat16),
            jax.ShapeDtypeStruct(forcing.shape, f32),
        ),
        in_specs=[pl.BlockSpec(memory_space=vmem)] * 2,
        out_specs=(pl.BlockSpec(memory_space=pl.ANY),) * 2,
        scratch_shapes=[dma((2,))],
        name="write_out",
    )(*[pltpu.with_memory_space_constraint(x, vmem) for x in held])


def solution(mesh):
    return jax.shard_map(
        local,
        mesh=mesh,
        in_specs=(
            P(None, None, "yb", "xb"),
            P(None, None, "yb", "xb"),
            P("yb", "xb"),
            P("yb", "xb"),
            P("yb", "xb"),
            P("yb", "xb"),
        ),
        out_specs=(P(None, None, "yb", "xb"), P("yb", "xb")),
        check_vma=False,
    )
```

```python
import functools

import jax
import jax.numpy as jnp
from jax import lax
from jax.experimental import pallas as pl
from jax.experimental.pallas import tpu as pltpu
from jax.sharding import PartitionSpec as P

ITERS = 3
MESH = pl.DeviceIdType.MESH
SHIFT = 4.1
SCALE = 4.0
DIRECT = 64
NORTH, SOUTH = 0, 1
LEFT, RIGHT = 0, 1
TEMP, DIFF, EASTWARD, NORTHWARD = range(4)


def add_up(terms):
    while len(terms) > 1:
        terms = [sum(terms[i:i + 2][1:], terms[i]) for i in range(0, len(terms), 2)]
    return terms[0]


def inner(a, b, moments):
    return add_up([x * y * moments[i + j] for i, x in enumerate(a) for j, y in enumerate(b)])


def cg_coefficients(moments):
    one = jnp.ones_like(moments[0])
    zero = jnp.zeros_like(one)
    height = [zero] * ITERS
    residual = [one]
    direction = [one]
    norm = moments[0]
    for step in range(ITERS):
        image = [SHIFT * d for d in direction] + [zero]
        for i, d in enumerate(direction):
            image[i + 1] = image[i + 1] + SCALE * d
        alpha = jnp.clip(norm / inner(direction, image, moments), 0.0, 10.0)
        for i, d in enumerate(direction):
            height[i] = height[i] + alpha * d
        if step + 1 < ITERS:
            padded = residual + [zero]
            residual = [p - alpha * m for p, m in zip(padded, image)]
            new = jnp.maximum(inner(residual, residual, moments), 0.0)
            beta = new / norm
            longer = direction + [zero]
            direction = [p + beta * d for p, d in zip(residual, longer)]
            norm = new
    return height


def kernel(
    nx, ny, levels,
    trac, vel, counts_in, lateral_in, vertical_in, forcing_in,
    rounded, out_height,
    wide, salt, counts_i, lateral, kv, force,
    strips, corners, y_send, late_send, x_recv, corner_recv, y_recv, late_recv,
    advected, values, ratios, inverses, parts,
    load_sem, send1, recv1, send_r, recv_r, ready,
):
    h, lanes = force.shape
    ext = h + 8
    slots = lanes // levels
    mid_level = levels // 2
    mx, my = lax.axis_index("xb"), lax.axis_index("yb")
    east, west = lax.rem(mx + 1, nx), lax.rem(mx + nx - 1, nx)
    north, south = lax.rem(my + 1, ny), lax.rem(my + ny - 1, ny)

    direct = nx * ny <= DIRECT
    me = my * nx + mx

    barrier = pltpu.get_barrier_semaphore()
    near = [(north, mx), (south, mx)]
    far = [(lax.rem(my + d, ny), mx) for d in range(2, ny - 1)]
    peers = near + [(my, lax.rem(mx + d, nx)) for d in range(1, nx)] + far
    own = pl.ds(0, h)
    loads = [
        pltpu.make_async_copy(trac.at[0], wide.at[TEMP, :, own, :], load_sem.at[0]),
        pltpu.make_async_copy(trac.at[1], salt, load_sem.at[1]),
        pltpu.make_async_copy(vel, wide.at[pl.ds(EASTWARD, 2), :, own, :], load_sem.at[2]),
        pltpu.make_async_copy(counts_in, counts_i, load_sem.at[3]),
        pltpu.make_async_copy(lateral_in, lateral, load_sem.at[4]),
        pltpu.make_async_copy(vertical_in, kv, load_sem.at[5]),
        pltpu.make_async_copy(forcing_in, force, load_sem.at[6]),
    ]
    for load in loads:
        load.start()
    for y, x in peers:
        pl.semaphore_signal(barrier, inc=1, device_id={"xb": x, "yb": y}, device_id_type=MESH)

    def clear(side):
        y_recv[side] = jnp.zeros(y_recv.shape[1:], jnp.float32)
        late_recv[side] = jnp.zeros(late_recv.shape[1:], jnp.float32)
        for i in (LEFT, RIGHT):
            corner_recv[i, side] = jnp.zeros(corner_recv.shape[2:], jnp.float32)

    pl.when(my == ny - 1)(lambda: clear(NORTH))
    pl.when(my == 0)(lambda: clear(SOUTH))
    for load in loads:
        load.wait()

    def lroll(x, shift):
        return pltpu.roll(x, shift % lanes, 1)

    def up(x):
        return pltpu.roll(x, x.shape[0] - 1, 0)

    def down(x):
        return pltpu.roll(x, 1, 0)

    def turn(x):
        return pltpu.roll(x, 4, 0)

    def spread(x):
        shift = slots
        while shift < lanes:
            x = x + lroll(x, shift)
            shift *= 2
        return x

    half = lax.broadcasted_iota(jnp.int32, (8, lanes), 0) < 4
    fourth = lax.broadcasted_iota(jnp.int32, (8, lanes), 0) == 3
    lane = lax.broadcasted_iota(jnp.int32, (h, lanes), 1)
    slot = lane % slots
    group = lane // slots
    gap = (slot < 2) | (slot >= 6)
    n_own = counts_i[...].astype(jnp.float32)
    h_own = lateral[...]
    f_own = force[...]
    face_e = jnp.minimum(n_own, lroll(n_own, -1))
    face_low = jnp.minimum(n_own[:8], up(n_own[:8]))

    def low_pair(a, b):
        return jnp.where(half, a[:8], turn(b[:8]))

    def high_pair(a, b):
        return jnp.where(half, turn(b[h - 8:]), a[h - 8:])

    pack = [jnp.zeros((h, lanes), jnp.float32)] * 4
    lows = []
    for k in range(levels):
        t = wide[TEMP, k, 0:h, :]
        u = wide[EASTWARD, k, 0:h, :]
        v = wide[NORTHWARD, k, 0:h, :]
        d = salt[k] - t
        wide[DIFF, k, 0:h, :] = d
        flux = jnp.maximum(u, 0.0) * d + jnp.minimum(u, 0.0) * lroll(d, -1)
        u_out = jnp.where(lane == 3, jnp.where(k < face_e, flux, 0.0), u)
        here = group == k
        for i, x in enumerate((t, d, u_out, v)):
            pack[i] = jnp.where(here, lroll(x, slots * k + 4), pack[i])
        flux = jnp.maximum(v[:8], 0.0) * d[:8] + jnp.minimum(v[:8], 0.0) * up(d[:8])
        v_low = jnp.where(fourth, jnp.where(k < face_low, flux, 0.0), v[:8])
        y_send[NORTH, k] = low_pair(d, u)
        lows.append(v_low)
        y_send[SOUTH, k] = high_pair(d, u)
        if k >= mid_level:
            i = k - mid_level
            y_send[NORTH, levels + i] = low_pair(lows[i], v_low)
            y_send[SOUTH, levels + i] = high_pair(wide[NORTHWARD, i, 0:h, :], v)
            late_send[NORTH, i] = low_pair(wide[TEMP, i, 0:h, :], t)
            late_send[SOUTH, i] = high_pair(wide[TEMP, i, 0:h, :], t)
    t_own, d_own, u_edge, v_edge = pack
    for i, x in enumerate((n_own, h_own, f_own)):
        a, b = slots * i, slots * (i + 3)
        t_own = jnp.where((group == i) & gap, lroll(x, a + 4), t_own)
        t_own = jnp.where((group == i + 3) & (slot < 2), lroll(x, b + 2), t_own)
        t_own = jnp.where((group == i + 3) & (slot >= 6), lroll(x, b + 6), t_own)
    n_edge = spread(jnp.where(lane < slots, lroll(n_own, 4), 0.0))
    h_edge = spread(jnp.where(lane < slots, lroll(h_own, 4), 0.0))
    western = slot < 4
    sent = [
        [jnp.where(western, d_own, lroll(u_edge, 4)), jnp.where(western, v_edge, lroll(t_own, 4))],
        [jnp.where(western, lroll(u_edge, -4), d_own), jnp.where(western, lroll(t_own, -4), v_edge)],
    ]
    for i, (a, b) in enumerate(sent):
        strips[i, 0] = a
        strips[i, 1] = b
        corners[i, NORTH] = low_pair(a, b)
        corners[i, SOUTH] = high_pair(a, b)
    extra = [(n_own, h_own), (f_own, t_own), (d_own, u_edge), (n_edge, h_edge)]
    for i, (a, b) in enumerate(extra):
        y_send[NORTH, levels + mid_level + i] = low_pair(a, b)
        y_send[SOUTH, levels + mid_level + i] = high_pair(a, b)

    pl.semaphore_wait(barrier, len(peers))

    def remote(src, dst, send, recv, i, y, x):
        return pltpu.make_async_remote_copy(
            src_ref=src, dst_ref=dst, send_sem=send.at[i], recv_sem=recv.at[i],
            device_id={"xb": x, "yb": y}, device_id_type=MESH,
        )

    for y, x in near:
        pl.semaphore_signal(ready.at[0], inc=1, device_id={"xb": x, "yb": y}, device_id_type=MESH)
    strip_copies = [
        remote(strips.at[0], x_recv.at[LEFT], send1, recv1, 0, my, east),
        remote(strips.at[1], x_recv.at[RIGHT], send1, recv1, 1, my, west),
    ]
    row_copies = [
        [remote(y_send.at[SOUTH], y_recv.at[SOUTH], send1, recv1, 2, north, mx)],
        [remote(y_send.at[NORTH], y_recv.at[NORTH], send1, recv1, 3, south, mx)],
    ]
    corner_copies = [
        [
            remote(corners.at[0, SOUTH], corner_recv.at[LEFT, SOUTH], send1, recv1, 4, north, east),
            remote(corners.at[1, SOUTH], corner_recv.at[RIGHT, SOUTH], send1, recv1, 5, north, west),
        ],
        [
            remote(corners.at[0, NORTH], corner_recv.at[LEFT, NORTH], send1, recv1, 6, south, east),
            remote(corners.at[1, NORTH], corner_recv.at[RIGHT, NORTH], send1, recv1, 7, south, west),
        ],
    ]
    late_copies = [
        [remote(late_send.at[SOUTH], late_recv.at[SOUTH], send1, recv1, 8, north, mx)],
        [remote(late_send.at[NORTH], late_recv.at[NORTH], send1, recv1, 9, south, mx)],
    ]

    def begin(northward, southward):
        @pl.when(my < ny - 1)
        def _():
            for copy in northward:
                copy.start()

        @pl.when(my > 0)
        def _():
            for copy in southward:
                copy.start()

    def finish(northward, southward):
        @pl.when(my < ny - 1)
        def _():
            for copy in northward:
                copy.wait_send()
            for copy in southward:
                copy.wait_recv()

        @pl.when(my > 0)
        def _():
            for copy in northward:
                copy.wait_recv()
            for copy in southward:
                copy.wait_send()

    begin(*row_copies)
    for copy in strip_copies:
        copy.start()
    if direct:
        for y, x in far:
            pl.semaphore_signal(ready.at[1], inc=1, device_id={"xb": x, "yb": y}, device_id_type=MESH)
    pl.semaphore_wait(ready.at[0], len(near))
    begin(*corner_copies)
    begin(*late_copies)

    coef = kv[...]
    zero = jnp.zeros_like(coef)
    previous_link = zero
    previous_ratio = zero
    for k in range(levels):
        link = jnp.where(k + 1.0 < n_own, coef, 0.0) if k + 1 < levels else zero
        inverse = 1.0 / (1.0 + previous_link + link - previous_link * previous_ratio)
        previous_ratio = link * inverse
        previous_link = link
        inverses[k] = inverse
        ratios[k] = previous_ratio

    finish(*row_copies)

    row = lax.broadcasted_iota(jnp.int32, (ext, lanes), 0)
    lane = lax.broadcasted_iota(jnp.int32, (ext, lanes), 1)
    slot = lane % slots
    group = lane // slots
    rank = group.astype(jnp.float32)
    western = slot < 4
    first_lane = lane == 0
    last_lane = lane == lanes - 1
    beyond = ((row >= h) & (row < h + 4) & (my == ny - 1)) | ((row >= h + 4) & (my == 0))

    def split(from_north, from_south):
        a = jnp.where(half, from_north, from_south)
        b = turn(jnp.where(half, from_south, from_north))
        return a, b

    def tall(main, halo):
        return jnp.concatenate([main, halo], axis=0)

    for k in range(levels):
        d, u = split(y_recv[NORTH, k], y_recv[SOUTH, k])
        wide[DIFF, k, h:ext, :] = d
        wide[EASTWARD, k, h:ext, :] = u
    for k in range(mid_level):
        a, b = split(y_recv[NORTH, levels + k], y_recv[SOUTH, levels + k])
        wide[NORTHWARD, k, h:ext, :] = a
        wide[NORTHWARD, mid_level + k, h:ext, :] = b
    first = levels + mid_level
    halo = [split(y_recv[NORTH, first + i], y_recv[SOUTH, first + i]) for i in range(len(extra))]
    n_main, h_main = tall(n_own, halo[0][0]), tall(h_own, halo[0][1])
    f_main, t_own = tall(f_own, halo[1][0]), tall(t_own, halo[1][1])
    d_own, u_own = tall(d_own, halo[2][0]), tall(u_edge, halo[2][1])
    n_edge, h_edge = tall(n_edge, halo[3][0]), tall(h_edge, halo[3][1])

    n_main = jnp.where(beyond, 0.0, n_main)
    n_edge = jnp.where(beyond, 0.0, n_edge)

    def upwind(speed, here, there):
        return jnp.maximum(speed, 0.0) * here + jnp.minimum(speed, 0.0) * there

    inner_e = jnp.where(last_lane, 0.0, jnp.minimum(n_main, lroll(n_main, -1)))
    inner_mix = 0.5 * (h_main + lroll(h_main, -1))
    face_n = jnp.minimum(n_main, up(n_main))
    mix_n = 0.5 * (h_main + up(h_main))
    above = row == h + 3
    column = jnp.zeros((ext, lanes), jnp.float32)
    passed_e, passed_n, a_own = column, column, column
    for k in range(levels):
        d = wide[DIFF, k]
        flux_e = upwind(jnp.where(k < inner_e, wide[EASTWARD, k], 0.0), d, lroll(d, -1))
        v = wide[NORTHWARD, k]
        flux_n = jnp.where(above, v, upwind(jnp.where(k < face_n, v, 0.0), d, up(d)))
        adv = jnp.where(k < n_main, d - (flux_e - lroll(flux_e, 1) + flux_n - down(flux_n)), 0.0)
        advected[k] = adv
        column = column + adv
        passed_e = passed_e + jnp.where(k < inner_e, lroll(adv, -1) - adv, 0.0)
        passed_n = passed_n + jnp.where(k < face_n, up(adv) - adv, 0.0)
        a_own = jnp.where(group == k, lroll(adv, slots * k + 4), a_own)
    flow_e = inner_mix * passed_e
    flow_n = mix_n * passed_n
    mixed_main = column + (flow_e - lroll(flow_e, 1)) + (flow_n - down(flow_n))

    third, fourth = slot == 3, slot == 4
    coef_own = jnp.where(rank < jnp.minimum(n_edge, lroll(n_edge, -1)), 0.5 * (h_edge + lroll(h_edge, -1)), 0.0)
    coef_own_n = jnp.where(rank < jnp.minimum(n_edge, up(n_edge)), 0.5 * (h_edge + up(h_edge)), 0.0)

    for copy in strip_copies:
        copy.wait()
    finish(*corner_copies)

    x1, x2 = [], []
    for i in (LEFT, RIGHT):
        a, b = split(corner_recv[i, NORTH], corner_recv[i, SOUTH])
        x1.append(tall(x_recv[i, 0], a))
        x2.append(tall(x_recv[i, 1], b))
    d_side = jnp.where(western, x1[LEFT], x1[RIGHT])
    v_side = jnp.where(western, x2[LEFT], x2[RIGHT])
    u_side = jnp.where(western, lroll(x1[LEFT], -4), lroll(x1[RIGHT], 4))
    t_side = jnp.where(western, lroll(x2[LEFT], -4), lroll(x2[RIGHT], 4))
    fields = jnp.where((slot < 2) | (slot >= 6), t_side, 0.0)
    fields = jnp.where((slot == 2) | (slot == 3), lroll(t_side, 2 - 3 * slots), fields)
    fields = jnp.where((slot == 4) | (slot == 5), lroll(t_side, -2 - 3 * slots), fields)
    n_side = spread(jnp.where((group == 0) & ~beyond, fields, 0.0))
    h_side = spread(jnp.where(group == 1, fields, 0.0))
    f_far = lroll(fields, -2 * slots - 4)
    n_far, h_far = lroll(n_side, -4), lroll(h_side, -4)

    def to_east(x, y):
        a, b = lroll(x, -1), lroll(y, -1)
        return jnp.where(last_lane, b, a), jnp.where(last_lane, a, b)

    def to_west(x, y):
        a, b = lroll(x, 1), lroll(y, 1)
        return jnp.where(first_lane, b, a), jnp.where(first_lane, a, b)

    n_pair, h_pair = (n_main, n_far), (h_main, h_far)
    face_pair = [jnp.minimum(a, b) for a, b in zip(n_pair, to_east(*n_pair))]

    def from_east(x, edge):
        return lroll(jnp.where(fourth, edge, x), -1)

    face_side = jnp.minimum(n_side, from_east(n_side, n_edge))
    face_edge = jnp.minimum(n_edge, lroll(n_side, -1))
    face_up = jnp.minimum(n_side, up(n_side))
    open_side = jnp.where(rank < face_side, u_side, 0.0)
    open_edge = jnp.where(rank < face_edge, u_own, 0.0)
    open_up = jnp.where(rank < face_up, v_side, 0.0)

    def advect_side(c, edge):
        flux = upwind(open_side, c, from_east(c, edge))
        flux_edge = upwind(open_edge, edge, lroll(c, -1))
        return flux, flux_edge, upwind(open_up, c, up(c))

    def finish_side(c, flux, flux_edge, flux_n):
        flux_w = lroll(jnp.where(third, flux_edge, flux), 1)
        adv = jnp.where(rank < n_side, c - (flux - flux_w + flux_n - down(flux_n)), 0.0)
        return adv, jnp.where(third, flux_edge, jnp.where(fourth, lroll(flux, 1), 0.0))

    flux, flux_edge, flux_n = advect_side(d_side, d_own)
    flux = jnp.where(slot == slots - 1, u_side, flux)
    adv_side, faces_d = finish_side(d_side, flux, flux_edge, flux_n)

    coef_e = jnp.where(rank < face_side, 0.5 * (h_side + from_east(h_side, h_edge)), 0.0)
    coef_edge = jnp.where(rank < face_edge, 0.5 * (h_edge + lroll(h_side, -1)), 0.0)
    coef_n = jnp.where(rank < face_up, 0.5 * (h_side + up(h_side)), 0.0)
    gained = jnp.where(rank < n_edge, jnp.where(third, -faces_d, faces_d), 0.0)
    a_own = a_own + gained
    flow_e = coef_e * (from_east(adv_side, a_own) - adv_side)
    flow_edge = coef_edge * (lroll(adv_side, -1) - a_own)
    flow_w = lroll(jnp.where(third, flow_edge, flow_e), 1)
    flow_n = coef_n * (up(adv_side) - adv_side)
    mixed = adv_side + (flow_e - flow_w) + (flow_n - down(flow_n))
    inner = coef_own * jnp.where(slot == 2, lroll(gained, -1), jnp.where(fourth, -gained, 0.0))
    flow_w = lroll(jnp.where(third, flow_e, inner), 1)
    flow_n = coef_own_n * (up(gained) - gained)
    mixed_own = gained + (jnp.where(third, flow_edge, inner) - flow_w) + (flow_n - down(flow_n))
    rhs_far = lroll(spread(mixed), -4)
    added = lroll(spread(mixed_own), -4)
    rhs_main = f_main + (mixed_main + jnp.where((lane >= lanes - 2) | (lane < 2), added, 0.0)) / levels
    rhs_far = f_far + rhs_far / levels

    scale = 1.0 / (levels * SCALE)
    deep = [scale * x for x in n_pair]
    deep_e = [scale * x for x in face_pair]
    deep_w = to_west(*deep_e)
    deep_n = [jnp.minimum(a, up(a)) for a in deep]
    deep_s = [down(a) for a in deep_n]
    base = (0.1 - SHIFT) / SCALE
    centre = [base + ((a + b) + (c + d)) for a, b, c, d in zip(deep_e, deep_w, deep_n, deep_s)]

    def apply(field):
        at_e, at_w = to_east(*field), to_west(*field)
        return tuple(
            centre[i] * field[i] - deep_e[i] * at_e[i] - deep_w[i] * at_w[i]
            - deep_n[i] * up(field[i]) - deep_s[i] * down(field[i])
            for i in range(2)
        )

    v0 = (rhs_main, rhs_far)
    v1 = apply(v0)
    v2 = apply(v1)
    basis = [x[0][:h] for x in (v0, v1, v2)]
    step_e = v2[0] - to_east(*v2)[0]
    step_n = v2[0] - up(v2[0])
    energy = base * (v2[0] * v2[0]) + deep_e[0] * (step_e * step_e) + deep_n[0] * (step_n * step_n)
    products = [basis[m // 2] * basis[m - m // 2] for m in range(2 * ITERS - 1)] + [energy[:h]]
    rows = [jnp.sum(x, axis=0, keepdims=True) for x in products]
    rows.append(jnp.zeros((8 - len(rows), lanes), jnp.float32))
    part = jnp.concatenate(rows, axis=0)
    place = lax.broadcasted_iota(jnp.int32, (8, lanes), 1)
    part = jnp.sum(part, axis=1, keepdims=True)
    part = jnp.where(place == lax.broadcasted_iota(jnp.int32, (8, lanes), 0), part, 0.0)
    part = jnp.sum(part, axis=0, keepdims=True)

    def tracer_stage():
        finish(*late_copies)
        for k in range(mid_level):
            a, b = split(late_recv[NORTH, k], late_recv[SOUTH, k])
            wide[TEMP, k, h:ext, :] = a
            wide[TEMP, mid_level + k, h:ext, :] = b
        flux, flux_edge, flux_n = advect_side(t_side, t_own)
        adv_t, faces_t = finish_side(t_side, flux, flux_edge, flux_n)
        mix_pair = [0.5 * (a + b) for a, b in zip(h_pair, to_east(*h_pair))]
        face_e, mix_e = face_pair[0], mix_pair[0]
        rim = first_lane | last_lane
        swapped = [jnp.where(third, lroll(x, -1), lroll(x, 1)) for x in (adv_t, adv_side)]
        face_w = to_west(*face_pair)[0][:h]
        mix_w = to_west(*mix_pair)[0][:h]
        mix_s = down(mix_n)[:h]
        face_s = down(face_n)[:h]
        last, first = last_lane[:h], first_lane[:h]
        previous_link = zero
        previous = [zero, zero]
        for k in range(levels):
            t = wide[TEMP, k]
            speed = jnp.where(k < face_e, wide[EASTWARD, k], 0.0)
            edge = lroll(faces_t, -(slots * k + 4))
            flux_e = jnp.where(last_lane, edge, upwind(speed, t, lroll(t, -1)))
            flux_w = jnp.where(first_lane, edge, lroll(flux_e, 1))
            flux_n = upwind(jnp.where(k < face_n, wide[NORTHWARD, k], 0.0), t, up(t))
            adv_main = jnp.where(k < n_main, t - (flux_e - flux_w + flux_n - down(flux_n)), 0.0)
            ce = jnp.where(k < face_e[:h], mix_e[:h], 0.0)
            cw = jnp.where(k < face_w, mix_w, 0.0)
            cn = jnp.where(k < face_n[:h], mix_n[:h], 0.0)
            cs = jnp.where(k < face_s, mix_s, 0.0)
            keep = 1.0 - ((ce + cw) + (cn + cs))
            adv_d = jnp.where(rim, lroll(a_own, -(slots * k + 4)), advected[k])
            for i, adv in enumerate((adv_main, adv_d)):
                mid = adv[:h]
                edge = lroll(swapped[i][:h], -(slots * k + 4))
                at_e = jnp.where(last, edge, lroll(mid, -1))
                at_w = jnp.where(first, edge, lroll(mid, 1))
                mixed = keep * mid + ce * at_e + cw * at_w + cn * up(adv)[:h] + cs * down(adv)[:h]
                previous[i] = (mixed + previous_link * previous[i]) * inverses[k]
                values[i, k] = previous[i]
            previous_link = jnp.where(k + 1.0 < n_own, coef, 0.0)
        result = previous
        for k in range(levels - 1, -1, -1):
            if k + 1 < levels:
                result = [values[i, k] + ratios[k] * result[i] for i in range(2)]
            rounded[0, k] = result[0].astype(jnp.bfloat16)
            rounded[1, k] = (result[0] + result[1]).astype(jnp.bfloat16)

    if direct:
        parts[me] = part
        pl.semaphore_wait(ready.at[1], len(far))
        copies = []
        for dy in range(ny):
            for dx in range(nx):
                if dx or dy:
                    y, x = lax.rem(my + dy, ny), lax.rem(mx + dx, nx)
                    copies.append(remote(parts.at[me], parts.at[me], send_r, recv_r, 0, y, x))
        for copy in copies:
            copy.start()
        tracer_stage()
        others = pl.ds(0, nx * ny - 1)
        remote(parts.at[others], parts.at[others], send_r, recv_r, 0, north, mx).wait()
        total = add_up([parts[i] for i in range(nx * ny)])
    else:
        parts[mx] = part
        copies = []
        for d in range(1, nx):
            copies.append(remote(parts.at[mx], parts.at[mx], send_r, recv_r, d, my, lax.rem(mx + d, nx)))
        for copy in copies:
            copy.start()
        for copy in copies:
            copy.wait()
        mine = nx + my
        parts[mine] = add_up([parts[i] for i in range(nx)])
        copies = []
        for d in range(1, ny):
            copies.append(remote(parts.at[mine], parts.at[mine], send_r, recv_r, nx + d, lax.rem(my + d, ny), mx))
        for copy in copies:
            copy.start()
        tracer_stage()
        for copy in copies:
            copy.wait()
        total = add_up([parts[nx + i] for i in range(ny)])
    moments = [
        jnp.sum(jnp.where(place[:1] == m, total, 0.0), axis=1, keepdims=True) for m in range(2 * ITERS)
    ]
    weights = cg_coefficients(moments)
    out_height[...] = sum(w * b for w, b in zip(weights, basis))


def write_out(rounded, height, out_tracers, out_height, sem):
    copies = [
        pltpu.make_async_copy(rounded, out_tracers, sem.at[0]),
        pltpu.make_async_copy(height, out_height, sem.at[1]),
    ]
    for copy in copies:
        copy.start()
    for copy in copies:
        copy.wait()


def local(tracers, velocities, level_counts, lateral_diffusivity, vertical_diffusivity, forcing):
    levels = tracers.shape[1]
    h, lanes = forcing.shape
    assert tracers.shape[0] == 2 and 8 * levels == lanes and h % 8 == 0
    nx, ny = lax.axis_size("xb"), lax.axis_size("yb")
    assert nx > 2 and ny > 2
    f32 = jnp.float32
    ext = h + 8
    slots = nx * ny if nx * ny <= DIRECT else nx + ny
    planes = levels + levels // 2 + 4
    dma = pltpu.SemaphoreType.DMA
    vmem = pltpu.VMEM
    held = pl.pallas_call(
        functools.partial(kernel, nx, ny, levels),
        out_shape=(vmem(tracers.shape, jnp.bfloat16), vmem(forcing.shape, f32)),
        in_specs=[pl.BlockSpec(memory_space=pl.ANY)] * 6,
        out_specs=(pl.BlockSpec(memory_space=vmem),) * 2,
        scratch_shapes=[
            vmem((4, levels, ext, lanes), f32),
            vmem((levels, h, lanes), f32),
            vmem((h, lanes), jnp.int32),
            vmem((h, lanes), f32),
            vmem((h, lanes), f32),
            vmem((h, lanes), f32),
            vmem((2, 2, h, lanes), f32),
            vmem((2, 2, 8, lanes), f32),
            vmem((2, planes, 8, lanes), f32),
            vmem((2, levels // 2, 8, lanes), f32),
            vmem((2, 2, h, lanes), f32),
            vmem((2, 2, 8, lanes), f32),
            vmem((2, planes, 8, lanes), f32),
            vmem((2, levels // 2, 8, lanes), f32),
            vmem((levels, ext, lanes), f32),
            vmem((2, levels, h, lanes), f32),
            vmem((levels, h, lanes), f32),
            vmem((levels, h, lanes), f32),
            vmem((slots, 1, lanes), f32),
            dma((7,)),
            dma((10,)), dma((10,)),
            dma((slots,)), dma((slots,)),
            pltpu.SemaphoreType.REGULAR((2,)),
        ],
        compiler_params=pltpu.CompilerParams(collective_id=0, has_side_effects=True),
        name="ocean_step",
    )(tracers, velocities, level_counts, lateral_diffusivity, vertical_diffusivity, forcing)
    return pl.pallas_call(
        write_out,
        out_shape=(
            jax.ShapeDtypeStruct(tracers.shape, jnp.bfloat16),
            jax.ShapeDtypeStruct(forcing.shape, f32),
        ),
        in_specs=[pl.BlockSpec(memory_space=vmem)] * 2,
        out_specs=(pl.BlockSpec(memory_space=pl.ANY),) * 2,
        scratch_shapes=[dma((2,))],
        name="write_out",
    )(*[pltpu.with_memory_space_constraint(x, vmem) for x in held])


def solution(mesh):
    return jax.shard_map(
        local,
        mesh=mesh,
        in_specs=(
            P(None, None, "yb", "xb"),
            P(None, None, "yb", "xb"),
            P("yb", "xb"),
            P("yb", "xb"),
            P("yb", "xb"),
            P("yb", "xb"),
        ),
        out_specs=(P(None, None, "yb", "xb"), P("yb", "xb")),
        check_vma=False,
    )
```
